128 devices in a mesh: gx: 16 (over z_hi, y, core), gy: 8 (over z_lo, x).
Axes of the slice: x: 4, y: 4, z: 4 (z_hi: 2, z_lo: 2; z = z_hi * 2 + z_lo), core: 2. Of those that a mesh axis runs over, the one named last changes fastest.
Arguments:
- slide_tokens: bfloat16 [128, 1024, 768], P('gy', 'gx'), may hold values from -9 to 9
- tissue: int32 [128, 1024], P('gy', 'gx'), may hold values 0 or 1
- grad_tokens: bfloat16 [128, 1024, 768], P('gy', 'gx'), may hold values from -6 to 6
- w_qkv: bfloat16 [768, 2304], replicated, may hold values from -1 to 1
- w_out: bfloat16 [768, 768], replicated, may hold values from -0.21875 to 0.21875
Outputs:
- block_out: bfloat16 [128, 1024, 768], P('gy', 'gx')
- grad_in: bfloat16 [128, 1024, 768], P('gy', 'gx')
- grad_wqkv: float32 [768, 2304], replicated
- grad_wout: float32 [768, 768], replicated
The draws below stay inside these ranges and needn't reach their ends.
All inputs are finite; a program needn't handle non-finite values. No bound on the sum of `tissue` on one device may be relied on, other than what follows from the above.
Results may differ from the reference program's by a relative error of at most 0.013.
Values may be sent and summed in bfloat16 or wider, within the bound.
No kernel may reach another device: no remote copies, remote signals or barrier semaphores. Data moves between devices by JAX's collectives and lax.ppermute only.
A program may use at most 256 MiB of HBM per device.

```python
import math
import jax
import jax.numpy as jnp
from jax import lax

D = 768
HEADS = 24
HEAD_DIM = 32
WIN = 8
SHIFT = 4
SLIDE_ROWS = 128
SLIDE_COLS = 1024


def drawn_signs(key):
    sign_bits = jax.random.randint(jax.random.fold_in(key, 9101), (D,), 0, 2)
    return (2 * sign_bits - 1).astype(jnp.float32)


def draw_slide_tokens(key, part):
    array_shape = (SLIDE_ROWS, SLIDE_COLS, D)
    noise_key = jax.random.fold_in(key, 9102)
    strength_key = jax.random.fold_in(key, 9103)
    noise_part = jax.random.truncated_normal(noise_key, -6.0, 6.0, array_shape, jnp.float32)
    strength = jax.random.uniform(strength_key, (SLIDE_ROWS, SLIDE_COLS, 1), jnp.float32, 1.0, 5.0)
    chosen_tokens = jax.random.randint(jax.random.fold_in(key, 9104), (SLIDE_ROWS, SLIDE_COLS, 1), 0, 64) == 0
    sign_vector = drawn_signs(key)
    planted = strength * sign_vector[None, None, :] + 0.5 * noise_part
    return jnp.where(chosen_tokens, planted, noise_part).astype(jnp.bfloat16)


def draw_w_qkv(key, part):
    base_key = jax.random.fold_in(key, 9105)
    base_part = jax.random.truncated_normal(base_key, -6.0, 6.0, (D, 3 * D), jnp.float32) * (1.0 / math.sqrt(D))
    head_pick = jax.random.randint(jax.random.fold_in(key, 9106), (), 0, HEADS)
    column = jnp.arange(3 * D)
    start_query = head_pick * HEAD_DIM
    in_query = jnp.logical_and(column >= start_query, column < start_query + HEAD_DIM)
    in_key = jnp.logical_and(column >= D + start_query, column < D + start_query + HEAD_DIM)
    plant_scale = math.sqrt(320.0 / (math.sqrt(HEAD_DIM) * D))
    added = plant_scale / math.sqrt(D) * drawn_signs(key)[:, None]
    return (base_part + jnp.where(jnp.logical_or(in_query, in_key)[None, :], added, 0.0)).astype(jnp.bfloat16)


def plant(drawn, key, least, largest):
    shape = drawn.shape
    place = [jax.random.randint(jax.random.fold_in(key, axis), (), 0, shape[axis]) for axis in range(len(shape))]
    drawn = drawn.at[tuple(place)].set(least)
    longest = shape.index(max(shape))
    place[longest] = (place[longest] + 1) % shape[longest]
    return drawn.at[tuple(place)].set(largest)


def block_levels(own_key, dims, cuts, smallest, largest):
    gain = 1.0
    for dim, blocks in cuts:
        draws = jax.random.uniform(jax.random.fold_in(jax.random.fold_in(own_key, 6), dim), (blocks,), jnp.float32, smallest / len(cuts), largest / len(cuts))
        gain = gain * jnp.repeat(jnp.exp(draws), dims[dim] // blocks).reshape((-1,) + (1,) * (len(dims) - 1 - dim))
    return gain


def gaussian(own_key, extent, deviation, reach, cuts=(), kind=jnp.bfloat16):
    values = jax.random.normal(own_key, extent, jnp.float32) * deviation
    if len(cuts) > 0:
        values = block_levels(own_key, extent, cuts, -0.22, 0.18) * values
    return jnp.clip(values, min=-reach, max=reach).astype(kind)


def setup_inputs(seed: int = 0) -> dict:
    key_of = jax.random.split(jax.random.key(seed), 6)
    slide_tokens = draw_slide_tokens(jax.random.fold_in(key_of[5], 71), 0)
    tissue = plant((jax.random.randint(key_of[1], (SLIDE_ROWS, SLIDE_COLS), 0, 4) < 3).astype(jnp.int32), jax.random.fold_in(key_of[1], 1), 0, 1)
    grad_tokens = gaussian(key_of[2], (SLIDE_ROWS, SLIDE_COLS, D), 1.0, 6.0, ((0, 8), (1, 16)))
    w_qkv = draw_w_qkv(jax.random.fold_in(key_of[5], 71), 0)
    w_out = gaussian(key_of[4], (D, D), D ** -0.5, 0.21875)
    return dict(slide_tokens=slide_tokens, tissue=tissue, grad_tokens=grad_tokens, w_qkv=w_qkv, w_out=w_out)


epsilon = 1e-05

def windows(tensor):
    row_count, col_count, feature_dim = tensor.shape
    tensor = tensor.reshape(row_count // WIN, WIN, col_count // WIN, WIN, feature_dim)
    return tensor.transpose(0, 2, 1, 3, 4).reshape(-1, WIN * WIN, feature_dim)

def unwindows(tensor, row_count, col_count):
    feature_dim = tensor.shape[-1]
    tensor = tensor.reshape(row_count // WIN, col_count // WIN, WIN, WIN, feature_dim)
    return tensor.transpose(0, 2, 1, 3, 4).reshape(row_count, col_count, feature_dim)

def split_heads(tensor):
    return tensor.reshape(tensor.shape[0], tensor.shape[1], HEADS, -1)

def attend(qkv_win, keep_win):
    model_dim = qkv_win.shape[-1] // 3
    queries = split_heads(qkv_win[..., :model_dim])
    keys_part = split_heads(qkv_win[..., model_dim:2 * model_dim])
    values_part = split_heads(qkv_win[..., 2 * model_dim:])
    score_scale = 1.0 / math.sqrt(model_dim // HEADS)
    scores = jnp.einsum('wqhd,wkhd->whqk', queries, keys_part, preferred_element_type=jnp.float32) * score_scale
    win_tokens = qkv_win.shape[1]
    itself = jnp.eye(win_tokens, dtype=bool)
    allowed = jnp.logical_or(keep_win[:, None, None, :] > 0.5, itself[None, None])
    scores = jnp.where(allowed, scores, -1e+30)
    maximum = lax.optimization_barrier(jnp.max(scores, -1, keepdims=True))
    exponent = jnp.exp(scores - maximum)
    attn_probs = exponent / lax.optimization_barrier(jnp.sum(exponent, -1, keepdims=True))
    weights_half = attn_probs.astype(jnp.bfloat16)
    mixed_out = jnp.einsum('whqk,wkhd->wqhd', weights_half, values_part, preferred_element_type=jnp.float32).astype(jnp.bfloat16)
    return (mixed_out.reshape(qkv_win.shape[0], win_tokens, model_dim), attn_probs)

def attend_back(qkv_win, attn_probs, grad_mixed):
    model_dim = qkv_win.shape[-1] // 3
    window_count, win_tokens = (qkv_win.shape[0], qkv_win.shape[1])
    queries = split_heads(qkv_win[..., :model_dim])
    keys_part = split_heads(qkv_win[..., model_dim:2 * model_dim])
    values_part = split_heads(qkv_win[..., 2 * model_dim:])
    score_scale = 1.0 / math.sqrt(model_dim // HEADS)
    grad_heads = split_heads(grad_mixed)
    grad_prob = jnp.einsum('wqhd,wkhd->whqk', grad_heads, values_part, preferred_element_type=jnp.float32)
    weights_half = attn_probs.astype(jnp.bfloat16)
    grad_value = jnp.einsum('whqk,wqhd->wkhd', weights_half, grad_heads, preferred_element_type=jnp.float32).astype(jnp.bfloat16)
    grad_score = attn_probs * (grad_prob - lax.optimization_barrier(jnp.sum(grad_prob * attn_probs, -1, keepdims=True))) * score_scale
    score_half = grad_score.astype(jnp.bfloat16)
    grad_query = jnp.einsum('whqk,wkhd->wqhd', score_half, keys_part, preferred_element_type=jnp.float32).astype(jnp.bfloat16)
    grad_key = jnp.einsum('whqk,wqhd->wkhd', score_half, queries, preferred_element_type=jnp.float32).astype(jnp.bfloat16)
    shape_out = (window_count, win_tokens, model_dim)
    return jnp.concatenate([grad_query.reshape(shape_out), grad_key.reshape(shape_out), grad_value.reshape(shape_out)], -1)

def layer_region(shifted, keep_mask, grad_shift, owned_mask, w_qkv, w_out):
    row_count, col_count, model_dim = shifted.shape
    flat_in = shifted.reshape(-1, model_dim).astype(jnp.float32)
    centered = flat_in - lax.optimization_barrier(jnp.mean(flat_in, -1, keepdims=True))
    inv_sigma = lax.rsqrt(lax.optimization_barrier(jnp.mean(centered * centered, -1, keepdims=True)) + epsilon)
    normed = centered * inv_sigma
    hidden = normed.astype(jnp.bfloat16)
    qkv = jnp.dot(hidden, w_qkv, preferred_element_type=jnp.float32).astype(jnp.bfloat16)
    qkv_win = windows(qkv.reshape(row_count, col_count, -1))
    keep_win = windows(keep_mask[..., None])[..., 0]
    mixed_out, attn_probs = attend(qkv_win, keep_win)
    mixed_flat = unwindows(mixed_out, row_count, col_count).reshape(-1, model_dim)
    output = jnp.dot(mixed_flat, w_out, preferred_element_type=jnp.float32).astype(jnp.bfloat16)
    grad_flat = grad_shift.reshape(-1, model_dim)
    grad_mixed = jnp.dot(grad_flat, w_out.T, preferred_element_type=jnp.float32).astype(jnp.bfloat16)
    grad_qkv = attend_back(qkv_win, attn_probs, windows(grad_mixed.reshape(row_count, col_count, model_dim)))
    grad_qkv = unwindows(grad_qkv, row_count, col_count).reshape(-1, 3 * model_dim)
    own_column = owned_mask.reshape(-1, 1).astype(jnp.bfloat16)
    contract = (((0,), (0,)), ((), ()))
    grad_wout = lax.dot_general(mixed_flat * own_column, grad_flat, contract, preferred_element_type=jnp.float32)
    grad_wqkv = lax.dot_general(hidden * own_column, grad_qkv, contract, preferred_element_type=jnp.float32)
    grad_hidden = jnp.dot(grad_qkv, w_qkv.T, preferred_element_type=jnp.float32)
    grad_shifted = inv_sigma * (grad_hidden - lax.optimization_barrier(jnp.mean(grad_hidden, -1, keepdims=True)) - normed * lax.optimization_barrier(jnp.mean(grad_hidden * normed, -1, keepdims=True)))
    shape_out = (row_count, col_count, model_dim)
    return (output.reshape(shape_out), grad_shifted.astype(jnp.bfloat16).reshape(shape_out), grad_wqkv, grad_wout)

def reference(slide_tokens, tissue, grad_tokens, w_qkv, w_out):
    row_count, col_count, model_dim = slide_tokens.shape
    shifted = jnp.roll(slide_tokens, (-SHIFT, -SHIFT), (0, 1))
    keep_mask = jnp.roll(tissue, (-SHIFT, -SHIFT), (0, 1)).astype(jnp.float32)
    grad_shift = jnp.roll(grad_tokens, (-SHIFT, -SHIFT), (0, 1))
    band_count = row_count // WIN
    band_x = shifted.reshape(band_count, WIN, col_count, model_dim)
    band_k = keep_mask.reshape(band_count, WIN, col_count)
    band_g = grad_shift.reshape(band_count, WIN, col_count, model_dim)

    def band_step(totals, pieces):
        piece_x, piece_k, piece_g = pieces
        output, grad_part, part_qkv, part_out = layer_region(piece_x, piece_k, piece_g, jnp.ones(piece_k.shape, jnp.float32), w_qkv, w_out)
        return ((totals[0] + part_qkv, totals[1] + part_out), (output, grad_part))
    start = (jnp.zeros((model_dim, 3 * model_dim), jnp.float32), jnp.zeros((model_dim, model_dim), jnp.float32))
    totals, stacked = lax.scan(band_step, start, (band_x, band_k, band_g))
    attn_all = stacked[0].reshape(row_count, col_count, model_dim)
    grad_all = stacked[1].reshape(row_count, col_count, model_dim)
    block_out = (slide_tokens.astype(jnp.float32) + jnp.roll(attn_all, (SHIFT, SHIFT), (0, 1)).astype(jnp.float32)).astype(jnp.bfloat16)
    grad_in = (grad_tokens.astype(jnp.float32) + jnp.roll(grad_all, (SHIFT, SHIFT), (0, 1)).astype(jnp.float32)).astype(jnp.bfloat16)
    return (block_out, grad_in, totals[0], totals[1])
```

```python
import functools
import math
import jax
import jax.numpy as jnp
from jax import lax
from jax.experimental import pallas as pl
from jax.experimental.pallas import tpu as pltpu
from jax.sharding import PartitionSpec as P

HEADS = 24
WIN = 8
SHIFT = 4
D = 768
GD = 256
EPS = 1e-05
SCALE = 1.0 / math.sqrt(32)
LOG2E = math.log2(math.e)
NT = (((1,), (1,)), ((), ()))
NN = (((1,), (0,)), ((), ()))
F32 = jnp.float32
BF16 = jnp.bfloat16


def mm(a, b, dims=NN):
    return lax.dot_general(a, b, dims, preferred_element_type=F32)


def spread(t, head_lane):
    zero = jnp.zeros_like(t)
    return jnp.concatenate([jnp.where(head_lane == h, t, zero) for h in range(4)], 0)


def gather_diag(full, head_lane):
    out = full[0:64]
    for h in range(1, 4):
        out = jnp.where(head_lane == h, full[64 * h : 64 * h + 64], out)
    return out


def attn_body(nwin, x_ref, g_ref, bias_ref, wq_ref, wk_ref, wv_ref, wo_ref,
              mixed_ref, dq_ref, dk_ref, dv_ref, part_ref,
              hid, hid_t, qs, ks, vs, gm, mix_t):
    tokens = nwin * 64
    tile = 256

    @pl.when(pl.program_id(0) == 0)
    def _():
        @pl.loop(0, tokens // 128)
        def _(i):
            rows = pl.ds(pl.multiple_of(i * 128, 128), 128)
            x = x_ref[rows, :].astype(F32)
            c = x - jnp.mean(x, -1, keepdims=True)
            inv = lax.rsqrt(jnp.mean(c * c, -1, keepdims=True) + EPS)
            n = c * inv
            hid[rows, :] = n.astype(BF16)
            hid_t[:, rows] = jnp.transpose(n).astype(BF16)

    @pl.loop(0, tokens // tile)
    def _(i):
        rows = pl.ds(pl.multiple_of(i * tile, tile), tile)
        h = hid[rows, :]
        qs[rows, :] = mm(h, wq_ref[...]).astype(BF16)
        ks[rows, :] = mm(h, wk_ref[...]).astype(BF16)
        vs[rows, :] = mm(h, wv_ref[...]).astype(BF16)
        gm[rows, :] = mm(g_ref[rows, :], wo_ref[...], NT).astype(BF16)

    head_lane = lax.broadcasted_iota(jnp.int32, (64, 128), 1) // 32

    def chain(rows, lanes, bias):
        q, k, v, g = qs[rows, lanes], ks[rows, lanes], vs[rows, lanes], gm[rows, lanes]
        qb = spread(q, head_lane)
        gb = spread(g, head_lane)
        s = mm(k, qb, NT) * (SCALE * LOG2E) + bias
        e = jnp.exp2(s - jnp.max(s, 0, keepdims=True))
        p = e * (1.0 / jnp.sum(e, 0, keepdims=True))
        pb = p.astype(BF16)
        dp = mm(v, gb, NT)
        ds = p * ((dp - jnp.sum(dp * p, 0, keepdims=True)) * SCALE)
        db = ds.astype(BF16)
        dk_ref[rows, lanes] = mm(db, qb).astype(BF16)
        dv_ref[rows, lanes] = mm(pb, gb).astype(BF16)
        mixed_ref[rows, lanes] = gather_diag(mm(jnp.transpose(p).astype(BF16), v), head_lane).astype(BF16)
        dq_ref[rows, lanes] = gather_diag(mm(jnp.transpose(ds).astype(BF16), k), head_lane).astype(BF16)

    @pl.loop(0, nwin)
    def _(w):
        rows = pl.ds(pl.multiple_of(w * 64, 64), 64)
        b = bias_ref[rows, :]
        b = jnp.concatenate([b, b], 1)
        for s in range(GD // 128):
            chain(rows, slice(128 * s, 128 * s + 128), b)

    @pl.loop(0, tokens // 128)
    def _(i):
        rows = pl.ds(pl.multiple_of(i * 128, 128), 128)
        mix_t[:, rows] = jnp.transpose(mixed_ref[rows, :].astype(F32)).astype(BF16)

    @pl.loop(0, D // tile)
    def _(i):
        rows = pl.ds(pl.multiple_of(i * tile, tile), tile)
        h = hid_t[rows, :]
        part_ref[0, rows, 0:256] = mm(h, dq_ref[...]).astype(BF16)
        part_ref[0, rows, 256:512] = mm(h, dk_ref[...]).astype(BF16)
        part_ref[0, rows, 512:768] = mm(h, dv_ref[...]).astype(BF16)

    for j in range(3):
        cols = slice(256 * j, 256 * j + 256)
        part_ref[0, 768:1024, cols] = mm(mix_t[...], g_ref[:, cols]).astype(BF16)


def attn_call(x, g, bias, w_qkv, w_out):
    tokens = x.shape[0]
    nwin = tokens // 64
    whole = lambda i: (0, 0)
    cols = pl.BlockSpec((tokens, GD), lambda i: (0, i))
    wblock = lambda p: pl.BlockSpec((D, GD), lambda i: (0, 3 * p + i))
    tok = jax.ShapeDtypeStruct((tokens, D), BF16)
    return pl.pallas_call(
        functools.partial(attn_body, nwin),
        grid=(3,),
        in_specs=[
            pl.BlockSpec((tokens, D), whole),
            pl.BlockSpec((tokens, D), whole),
            pl.BlockSpec((tokens, 128), whole),
            wblock(0), wblock(1), wblock(2),
            pl.BlockSpec((GD, D), lambda i: (i, 0)),
        ],
        out_specs=[cols, cols, cols, cols, pl.BlockSpec((1, 1024, D), lambda i: (i, 0, 0))],
        out_shape=[tok, tok, tok, tok, jax.ShapeDtypeStruct((3, 1024, D), BF16)],
        scratch_shapes=[
            pltpu.VMEM((tokens, D), BF16),
            pltpu.VMEM((D, tokens), BF16),
            pltpu.VMEM((tokens, GD), BF16),
            pltpu.VMEM((tokens, GD), BF16),
            pltpu.VMEM((tokens, GD), BF16),
            pltpu.VMEM((tokens, GD), BF16),
            pltpu.VMEM((GD, tokens), BF16),
        ],
        compiler_params=pltpu.CompilerParams(
            dimension_semantics=("arbitrary",), vmem_limit_bytes=48 << 20
        ),
        cost_estimate=pl.CostEstimate(
            flops=14_000_000_000, bytes_accessed=20_000_000, transcendentals=1_600_000
        ),
        name="attention",
    )(x, g, bias, w_qkv, w_qkv, w_qkv, w_out)


def finish_body(x_ref, mixed_ref, dq_ref, dk_ref, dv_ref, wqkv_ref, wo_ref, attn_ref, gs_ref):
    attn_ref[...] = mm(mixed_ref[...], wo_ref[...]).astype(BF16)
    dh = mm(dq_ref[...], wqkv_ref[:, 0:768], NT)
    dh += mm(dk_ref[...], wqkv_ref[:, 768:1536], NT)
    dh += mm(dv_ref[...], wqkv_ref[:, 1536:2304], NT)
    x = x_ref[...].astype(F32)
    c = x - jnp.mean(x, -1, keepdims=True)
    inv = lax.rsqrt(jnp.mean(c * c, -1, keepdims=True) + EPS)
    n = c * inv
    back = dh - jnp.mean(dh, -1, keepdims=True) - n * jnp.mean(dh * n, -1, keepdims=True)
    gs_ref[...] = (inv * back).astype(BF16)


def finish_call(x, mixed, dq, dk, dv, w_qkv, w_out):
    tokens = x.shape[0]
    tile = 128
    t = pl.BlockSpec((tile, D), lambda i: (i, 0))
    tok = jax.ShapeDtypeStruct((tokens, D), BF16)
    return pl.pallas_call(
        finish_body,
        grid=(tokens // tile,),
        in_specs=[t, t, t, t, t,
                  pl.BlockSpec((D, 3 * D), lambda i: (0, 0), pipeline_mode=pl.Buffered(1)),
                  pl.BlockSpec((D, D), lambda i: (0, 0), pipeline_mode=pl.Buffered(1))],
        out_specs=[t, t],
        out_shape=[tok, tok],
        compiler_params=pltpu.CompilerParams(
            dimension_semantics=("arbitrary",), vmem_limit_bytes=32 << 20
        ),
        cost_estimate=pl.CostEstimate(
            flops=4_800_000_000, bytes_accessed=16_000_000, transcendentals=0
        ),
        name="finish",
    )(x, mixed, dq, dk, dv, w_qkv, w_out)


AXES = ("gx", "gy")


def place(i):
    gx, gy = divmod(i, 8)
    z_hi, y, core = gx // 8, gx // 2 % 4, gx % 2
    z_lo, x = divmod(gy, 4)
    return {"core": core, "x": x, "y": y, "z": 2 * z_hi + z_lo}


def number(d):
    z_hi, z_lo = divmod(d["z"], 2)
    return ((z_hi * 4 + d["y"]) * 2 + d["core"]) * 8 + z_lo * 4 + d["x"]


def exchange(v, axis, first):
    pairs = []
    for i in range(128):
        d = place(i)
        if axis == "core":
            d["core"] ^= 1
        elif (d["core"] == 0) == first:
            d[axis] ^= 1
        else:
            d[axis] = 3 - d[axis]
        pairs.append((i, number(d)))
    return lax.ppermute(v, AXES, pairs)


def half_of(axis, first):
    gx, gy = lax.axis_index("gx"), lax.axis_index("gy")
    core = gx % 2
    if axis == "core":
        return core
    p = {"x": gy % 4, "y": gx // 2 % 4, "z": gx // 8 * 2 + gy // 4}[axis]
    inner = ((p == 1) | (p == 2)).astype(jnp.int32)
    upper = (p >= 2).astype(jnp.int32)
    return jnp.where((core == 0) == first, inner, upper)


def add(a, b):
    return (a.astype(F32) + b.astype(F32)).astype(BF16)


def scatter_half(v, axis, first=True):
    n = v.shape[0] // 2
    b = half_of(axis, first)
    keep = lax.dynamic_slice_in_dim(v, b * n, n, 0)
    send = lax.dynamic_slice_in_dim(v, (1 - b) * n, n, 0)
    return add(keep, exchange(send, axis, first))


def gather_half(v, axis, first=True):
    b = half_of(axis, first)
    o = exchange(v, axis, first)
    return jnp.where(b == 0, jnp.concatenate([v, o], 0), jnp.concatenate([o, v], 0))


def total(parts):
    order = [["core"] + ["xyz"[(k + s) % 3] for s in range(3)] for k in range(3)]
    for s in range(4):
        parts = [scatter_half(p, o[s]) for p, o in zip(parts, order)]
    n = parts[0].shape[0]
    v = jnp.concatenate(parts, 0)
    v = scatter_half(v, "x", False)
    for axis in "yz":
        v = add(v, exchange(v, axis, False))
    v = gather_half(v, "x", False)
    parts = [v[n * k : n * k + n] for k in range(3)]
    for s in (3, 2, 1, 0):
        parts = [gather_half(p, o[s]) for p, o in zip(parts, order)]
    return parts


def neighbour(block, axis, distance):
    n = lax.axis_size(axis)
    return lax.ppermute(block, axis, [((i - distance) % n, i) for i in range(n)])


def windows(t):
    r, c, f = t.shape
    t = t.reshape(r // WIN, WIN, c // WIN, WIN, f)
    return t.transpose(0, 2, 1, 3, 4).reshape(r * c, f)


def unwindows(t, r, c):
    t = t.reshape(r // WIN, c // WIN, WIN, WIN, t.shape[-1])
    return t.transpose(0, 2, 1, 3, 4).reshape(r, c, t.shape[-1])


def local(slide_tokens, tissue, grad_tokens, w_qkv, w_out):
    rows, cols, _ = slide_tokens.shape
    keep = tissue.astype(BF16)
    xg = jnp.stack([slide_tokens, grad_tokens])
    below = neighbour(xg[:, :SHIFT], "gy", -1)
    below_k = neighbour(keep[:SHIFT], "gy", -1)
    xg = jnp.concatenate([xg[:, SHIFT:], below], 1)
    keep = jnp.concatenate([keep[SHIFT:], below_k], 0)
    right = neighbour(xg[:, :, :SHIFT], "gx", -1)
    right_k = neighbour(keep[:, :SHIFT], "gx", -1)
    xg = jnp.concatenate([xg[:, :, SHIFT:], right], 2)
    keep = jnp.concatenate([keep[:, SHIFT:], right_k], 1)

    x, g = windows(xg[0]), windows(xg[1])
    keep = windows(keep[..., None]).reshape(-1, 64, 1)
    lane = lax.broadcasted_iota(jnp.int32, (1, 64, 128), 2) % 64
    row = lax.broadcasted_iota(jnp.int32, (1, 64, 128), 1)
    bias = jnp.where((keep > 0.5) | (lane == row), 0.0, -1e30).astype(F32).reshape(-1, 128)
    mixed, dq, dk, dv, part = attn_call(x, g, bias, w_qkv, w_out)
    attn, grad = finish_call(x, mixed, dq, dk, dv, w_qkv, w_out)

    back = jnp.stack([unwindows(attn, rows, cols), unwindows(grad, rows, cols)])
    edge = cols - SHIFT
    left = neighbour(back[:, :, edge:], "gx", 1)
    back = jnp.concatenate([left, back[:, :, :edge]], 2)
    bottom = rows - SHIFT
    above = neighbour(back[:, bottom:], "gy", 1)
    back = jnp.concatenate([above, back[:, :bottom]], 1)
    block_out = add(slide_tokens, back[0])
    grad_in = add(grad_tokens, back[1])

    parts = total([part[k] for k in range(3)])
    whole = jnp.stack(parts).astype(F32)
    grad_wqkv = whole[:, :D].reshape(3, D, 3, GD).transpose(1, 2, 0, 3).reshape(D, 3 * D)
    grad_wout = whole[:, D:].reshape(D, D)
    return block_out, grad_in, grad_wqkv, grad_wout


def solution(mesh):
    tile = P("gy", "gx", None)
    return jax.shard_map(
        local,
        mesh=mesh,
        in_specs=(tile, P("gy", "gx"), tile, P(), P()),
        out_specs=(tile, tile, P(), P()),
        check_vma=False,
    )
```

```python
import functools
import math
import jax
import jax.numpy as jnp
from jax import lax
from jax.experimental import pallas as pl
from jax.experimental.pallas import tpu as pltpu
from jax.sharding import PartitionSpec as P

HEADS = 24
WIN = 8
SHIFT = 4
D = 768
GD = 256
EPS = 1e-05
SCALE = 1.0 / math.sqrt(32)
LOG2E = math.log2(math.e)
NT = (((1,), (1,)), ((), ()))
NN = (((1,), (0,)), ((), ()))
F32 = jnp.float32
BF16 = jnp.bfloat16


def mm(a, b, dims=NN):
    return lax.dot_general(a, b, dims, preferred_element_type=F32)


def spread(t, head_lane):
    zero = jnp.zeros_like(t)
    return jnp.concatenate([jnp.where(head_lane == h, t, zero) for h in range(4)], 0)


def gather_diag(full, head_lane):
    out = full[0:64]
    for h in range(1, 4):
        out = jnp.where(head_lane == h, full[64 * h : 64 * h + 64], out)
    return out


TOKENS = 1024
F = 2 * D + 128


def right_half(shape):
    return lax.broadcasted_iota(jnp.int32, shape, 1) >= 4


def seam(a, b):
    return jnp.where(right_half(a.shape), a, b)


def tile_of(t, j):
    return t[:, 8 * j : 8 * j + 8, :]


def pack_body(*refs):
    ins, (up, down, left, corner) = refs[:9], refs[9:]
    lane = 0
    for top, bottom, strip in (ins[0:3], ins[3:6], ins[6:9]):
        width = top.shape[-1]
        lanes = slice(lane, lane + width)
        lane += width
        for j in range(4):
            up[:, 8 * j : 8 * j + 8, lanes] = seam(tile_of(top, j), tile_of(top, j + 1))
        for j in range(3):
            down[:, 8 * j : 8 * j + 8, lanes] = seam(tile_of(bottom, j + 4), tile_of(bottom, j + 5))
        down[:, 24:32, lanes] = tile_of(bottom, 7)
        left[:, :, lanes] = strip[...]
        corner[:, :, lanes] = tile_of(bottom, 0)


def pack_call(x, g, kb):
    specs = []
    for t in (x, g, kb):
        w = t.shape[-1]
        specs += [
            pl.BlockSpec((4, 64, w), lambda i: (0, 0, 0)),
            pl.BlockSpec((4, 64, w), lambda i: (3, 0, 0)),
            pl.BlockSpec((16, 8, w), lambda i: (0, 0, 0)),
        ]
    shapes = [(4, 32, F), (4, 32, F), (16, 8, F), (4, 8, F)]
    return pl.pallas_call(
        pack_body,
        grid=(1,),
        in_specs=specs,
        out_specs=[pl.BlockSpec(sh, lambda i: (0, 0, 0)) for sh in shapes],
        out_shape=[jax.ShapeDtypeStruct(sh, BF16) for sh in shapes],
        compiler_params=pltpu.CompilerParams(vmem_limit_bytes=16 << 20),
        cost_estimate=pl.CostEstimate(flops=0, bytes_accessed=4_000_000, transcendentals=0),
        name="pack",
    )(x, x, x, g, g, g, kb, kb, kb)


def window_pieces(src, below, above, right, corner, lanes):
    out = []
    for j in range(8):
        nxt = tile_of(src[4:12], j + 1) if j < 7 else right[4:12, :, lanes]
        out.append(seam(tile_of(src[4:12], j), nxt))
    for j in range(4):
        own = seam(tile_of(src[12:16], j), tile_of(src[12:16], j + 1))
        out.append(jnp.concatenate([own, tile_of(below, j)[:, :, lanes]], 0))
    for j in range(4):
        nxt = tile_of(src[0:4], j + 5) if j < 3 else right[0:4, :, lanes]
        own = seam(tile_of(src[0:4], j + 4), nxt)
        top = tile_of(above, j)[:, :, lanes]
        if j == 3:
            top = seam(top, corner[:, :, lanes])
        out.append(jnp.concatenate([top, own], 0))
    return out


def attn_body(x_ref, g_ref, kb_ref, below, above, right, corner, wq_ref, wk_ref, wv_ref, wo_ref,
              mixed_ref, dq_ref, dk_ref, dv_ref, xw, part_ref,
              gw, bias, hid, hid_t, qs, ks, vs, gm, mix_t):

    @pl.when(pl.program_id(0) == 0)
    def _():
        halo = (below, above, right, corner)
        for w, t in enumerate(window_pieces(x_ref, *halo, slice(0, D))):
            xw[64 * w : 64 * w + 64, :] = t.astype(F32).reshape(64, D).astype(BF16)
        for w, t in enumerate(window_pieces(g_ref, *halo, slice(D, 2 * D))):
            gw[64 * w : 64 * w + 64, :] = t.astype(F32).reshape(64, D).astype(BF16)
        lane = lax.broadcasted_iota(jnp.int32, (64, 128), 1) % 64
        itself = lane == lax.broadcasted_iota(jnp.int32, (64, 128), 0)
        for w, t in enumerate(window_pieces(kb_ref, *halo, slice(2 * D, F))):
            keep = t.astype(F32).reshape(64, 128) > 0.5
            bias[64 * w : 64 * w + 64, :] = jnp.where(keep | itself, 0.0, -1e30)

        @pl.loop(0, TOKENS // 128)
        def _(i):
            rows = pl.ds(pl.multiple_of(i * 128, 128), 128)
            x = xw[rows, :].astype(F32)
            c = x - jnp.mean(x, -1, keepdims=True)
            inv = lax.rsqrt(jnp.mean(c * c, -1, keepdims=True) + EPS)
            n = c * inv
            hid[rows, :] = n.astype(BF16)
            hid_t[:, rows] = jnp.transpose(n).astype(BF16)

    @pl.loop(0, 1)
    def _(i):
        rows = pl.ds(0, TOKENS)
        h = hid[rows, :]
        qs[rows, :] = mm(h, wq_ref[...]).astype(BF16)
        ks[rows, :] = mm(h, wk_ref[...]).astype(BF16)
        vs[rows, :] = mm(h, wv_ref[...]).astype(BF16)
        gm[rows, :] = mm(gw[rows, :], wo_ref[...], NT).astype(BF16)

    head_lane = lax.broadcasted_iota(jnp.int32, (64, 128), 1) // 32

    U = 4
    TN = (((0,), (0,)), ((), ()))

    @pl.loop(0, 16 // U)
    def _(w):
        keys = []
        for u in range(U):
            rows = pl.ds(pl.multiple_of(w * 64 * U + 64 * u, 64), 64)
            for s in range(GD // 128):
                keys.append((rows, slice(128 * s, 128 * s + 128)))
        ch = [(qs[c], ks[c], vs[c], gm[c]) for c in keys]
        allow = []
        for u in range(U):
            bb = bias[keys[2 * u][0], :]
            allow += [jnp.concatenate([bb, bb], 1)] * 2
        qb = [spread(c[0], head_lane) for c in ch]
        sc = [mm(c[1], b, NT) for c, b in zip(ch, qb)]
        gb = [spread(c[3], head_lane) for c in ch]
        dp = [mm(c[2], b, NT) for c, b in zip(ch, gb)]
        ps, pbs, dbs = [], [], []
        for s, b in zip(sc, allow):
            s = s * (SCALE * LOG2E) + b
            e = jnp.exp2(s - jnp.max(s, 0, keepdims=True))
            p = e * (1.0 / jnp.sum(e, 0, keepdims=True))
            ps.append(p)
            pbs.append(p.astype(BF16))
        for p, d in zip(ps, dp):
            ds = p * ((d - jnp.sum(d * p, 0, keepdims=True)) * SCALE)
            dbs.append(ds.astype(BF16))
        dv = [mm(p, b) for p, b in zip(pbs, gb)]
        mx = [mm(p, c[2], TN) for p, c in zip(pbs, ch)]
        dk = [mm(d, b) for d, b in zip(dbs, qb)]
        dq = [mm(d, c[1], TN) for d, c in zip(dbs, ch)]
        for i, c in enumerate(keys):
            dv_ref[c] = dv[i].astype(BF16)
            mixed_ref[c] = gather_diag(mx[i], head_lane).astype(BF16)
            dk_ref[c] = dk[i].astype(BF16)
            dq_ref[c] = gather_diag(dq[i], head_lane).astype(BF16)

    @pl.loop(0, TOKENS // 128)
    def _(i):
        rows = pl.ds(pl.multiple_of(i * 128, 128), 128)
        mix_t[:, rows] = jnp.transpose(mixed_ref[rows, :].astype(F32)).astype(BF16)

    @pl.loop(0, 1)
    def _(i):
        rows = pl.ds(0, 768)
        h = hid_t[rows, :]
        part_ref[0, rows, 0:256] = mm(h, dq_ref[...]).astype(BF16)
        part_ref[0, rows, 256:512] = mm(h, dk_ref[...]).astype(BF16)
        part_ref[0, rows, 512:768] = mm(h, dv_ref[...]).astype(BF16)

    for j in range(3):
        cols = slice(256 * j, 256 * j + 256)
        part_ref[0, 768:1024, cols] = mm(mix_t[...], gw[:, cols]).astype(BF16)


def attn_call(x, g, kb, halo, w_qkv, w_out):
    fixed = lambda t: pl.BlockSpec(t.shape, lambda i: (0,) * t.ndim, pipeline_mode=pl.Buffered(1))
    cols = pl.BlockSpec((TOKENS, GD), lambda i: (0, i))
    wblock = lambda p: pl.BlockSpec((D, GD), lambda i: (0, 3 * p + i))
    tok = jax.ShapeDtypeStruct((TOKENS, D), BF16)
    return pl.pallas_call(
        attn_body,
        grid=(3,),
        in_specs=[fixed(t) for t in (x, g, kb, *halo)]
        + [wblock(0), wblock(1), wblock(2), pl.BlockSpec((GD, D), lambda i: (i, 0))],
        out_specs=[cols, cols, cols, cols, fixed(tok), pl.BlockSpec((1, 1024, D), lambda i: (i, 0, 0))],
        out_shape=[tok, tok, tok, tok, tok, jax.ShapeDtypeStruct((3, 1024, D), BF16)],
        scratch_shapes=[
            pltpu.VMEM((TOKENS, D), BF16),
            pltpu.VMEM((TOKENS, 128), F32),
            pltpu.VMEM((TOKENS, D), BF16),
            pltpu.VMEM((D, TOKENS), BF16),
            pltpu.VMEM((TOKENS, GD), BF16),
            pltpu.VMEM((TOKENS, GD), BF16),
            pltpu.VMEM((TOKENS, GD), BF16),
            pltpu.VMEM((TOKENS, GD), BF16),
            pltpu.VMEM((GD, TOKENS), BF16),
        ],
        compiler_params=pltpu.CompilerParams(
            dimension_semantics=("arbitrary",), vmem_limit_bytes=48 << 20
        ),
        cost_estimate=pl.CostEstimate(
            flops=14_000_000_000, bytes_accessed=20_000_000, transcendentals=1_600_000
        ),
        name="attention",
    )(x, g, kb, *halo, w_qkv, w_qkv, w_qkv, w_out)


def finish_body(x_ref, mixed_ref, dq_ref, dk_ref, dv_ref, wqkv_ref, wo_ref, attn_ref, gs_ref):
    attn_ref[...] = mm(mixed_ref[...], wo_ref[...]).astype(BF16)
    dh = mm(dq_ref[...], wqkv_ref[:, 0:768], NT)
    dh += mm(dk_ref[...], wqkv_ref[:, 768:1536], NT)
    dh += mm(dv_ref[...], wqkv_ref[:, 1536:2304], NT)
    x = x_ref[...].astype(F32)
    c = x - jnp.mean(x, -1, keepdims=True)
    inv = lax.rsqrt(jnp.mean(c * c, -1, keepdims=True) + EPS)
    n = c * inv
    back = dh - jnp.mean(dh, -1, keepdims=True) - n * jnp.mean(dh * n, -1, keepdims=True)
    gs_ref[...] = (inv * back).astype(BF16)


def finish_call(x, mixed, dq, dk, dv, w_qkv, w_out):
    tokens = x.shape[0]
    tile = 512
    t = pl.BlockSpec((tile, D), lambda i: (i, 0))
    tok = jax.ShapeDtypeStruct((tokens, D), BF16)
    return pl.pallas_call(
        finish_body,
        grid=(tokens // tile,),
        in_specs=[t, t, t, t, t,
                  pl.BlockSpec((D, 3 * D), lambda i: (0, 0), pipeline_mode=pl.Buffered(1)),
                  pl.BlockSpec((D, D), lambda i: (0, 0), pipeline_mode=pl.Buffered(1))],
        out_specs=[t, t],
        out_shape=[tok, tok],
        compiler_params=pltpu.CompilerParams(
            dimension_semantics=("arbitrary",), vmem_limit_bytes=32 << 20
        ),
        cost_estimate=pl.CostEstimate(
            flops=4_800_000_000, bytes_accessed=16_000_000, transcendentals=0
        ),
        name="finish",
    )(x, mixed, dq, dk, dv, w_qkv, w_out)


def merge_body(x_ref, g_ref, attn_ref, grad_ref, below, above, left, corner, out_ref, gin_ref):
    for src, win, dst, lanes in (
        (x_ref, attn_ref, out_ref, slice(0, D)),
        (g_ref, grad_ref, gin_ref, slice(D, 2 * D)),
    ):
        piece = lambda w: win[64 * w : 64 * w + 64, :].astype(F32).reshape(8, 8, D)
        far = lambda t, j: tile_of(t, j)[:, :, lanes].astype(F32)
        mids = [left[4:12, :, lanes].astype(F32)] + [piece(j) for j in range(8)]
        lows = [corner[:, :, lanes].astype(F32)] + [piece(8 + j)[0:4] for j in range(4)] + [far(below, j) for j in range(4)]
        tops = [left[0:4, :, lanes].astype(F32)] + [far(above, j) for j in range(4)] + [piece(12 + j)[4:8] for j in range(4)]
        for j in range(8):
            cols = slice(8 * j, 8 * j + 8)
            for rows, t in ((slice(4, 12), mids), (slice(12, 16), lows), (slice(0, 4), tops)):
                add = seam(t[j + 1], t[j])
                dst[rows, cols, :] = (src[rows, cols, :].astype(F32) + add).astype(BF16)


def merge_call(x, g, attn, grad, halo):
    tile = jax.ShapeDtypeStruct(x.shape, BF16)
    return pl.pallas_call(
        merge_body,
        out_shape=[tile, tile],
        compiler_params=pltpu.CompilerParams(vmem_limit_bytes=32 << 20),
        cost_estimate=pl.CostEstimate(flops=3_000_000, bytes_accessed=11_000_000, transcendentals=0),
        name="merge",
    )(x, g, attn, grad, *halo)


def split_body(attn_ref, grad_ref, up, down, side, corner):
    for win, lanes in ((attn_ref, slice(0, D)), (grad_ref, slice(D, 2 * D))):
        piece = lambda w: win[64 * w : 64 * w + 64, :].astype(F32).reshape(8, 8, D).astype(BF16)
        for j in range(4):
            cols = slice(8 * j, 8 * j + 8)
            up[:, cols, lanes] = piece(12 + j)[0:4]
            down[:, cols, lanes] = piece(8 + j)[4:8]
        side[0:4, :, lanes] = piece(15)[4:8]
        side[4:12, :, lanes] = piece(7)
        corner[:, :, lanes] = piece(15)[0:4]


def split_call(attn, grad):
    shapes = [(4, 32, 2 * D), (4, 32, 2 * D), (12, 8, 2 * D), (4, 8, 2 * D)]
    return pl.pallas_call(
        split_body,
        out_shape=[jax.ShapeDtypeStruct(sh, BF16) for sh in shapes],
        compiler_params=pltpu.CompilerParams(vmem_limit_bytes=16 << 20),
        cost_estimate=pl.CostEstimate(flops=0, bytes_accessed=5_000_000, transcendentals=0),
        name="split",
    )(attn, grad)


def widen_body(core_ref, *refs):
    own, other, (wqkv, wout) = refs[0:3], refs[3:6], refs[6:8]
    j = pl.program_id(0)
    here = core_ref[0]

    def put(srcs):
        rows = pl.ds(pl.multiple_of(j % 2 * 256, 256), 256)

        @pl.when(j < 3)
        def _():
            for k in range(3):
                for p in range(3):
                    wqkv[:, D * p + GD * k : D * p + GD * k + GD] = srcs[k][rows, GD * p : GD * p + GD].astype(F32)

        @pl.when(j == 3)
        def _():
            for k in range(3):
                wout[GD * k : GD * k + GD, :] = srcs[k][256:512, :].astype(F32)

    @pl.when(j // 2 == here)
    def _():
        put(own)

    @pl.when(j // 2 != here)
    def _():
        put(other)


def widen_call(core, own, other):
    half = pl.BlockSpec((512, D), lambda j, c: (0, 0), pipeline_mode=pl.Buffered(1))
    return pl.pallas_call(
        widen_body,
        grid_spec=pltpu.PrefetchScalarGridSpec(
            num_scalar_prefetch=1,
            grid=(4,),
            in_specs=[half] * 6,
            out_specs=[
                pl.BlockSpec((256, 3 * D), lambda j, c: (jnp.minimum(j, 2), 0)),
                pl.BlockSpec((D, D), lambda j, c: (0, 0)),
            ],
        ),
        out_shape=[jax.ShapeDtypeStruct((D, 3 * D), F32), jax.ShapeDtypeStruct((D, D), F32)],
        compiler_params=pltpu.CompilerParams(
            dimension_semantics=("arbitrary",), vmem_limit_bytes=32 << 20
        ),
        cost_estimate=pl.CostEstimate(flops=0, bytes_accessed=14_000_000, transcendentals=0),
        name="widen",
    )(core, *own, *other)

AXES = ("gx", "gy")


def place(i):
    gx, gy = divmod(i, 8)
    z_hi, y, core = gx // 8, gx // 2 % 4, gx % 2
    z_lo, x = divmod(gy, 4)
    return {"core": core, "x": x, "y": y, "z": 2 * z_hi + z_lo}


def number(d):
    z_hi, z_lo = divmod(d["z"], 2)
    return ((z_hi * 4 + d["y"]) * 2 + d["core"]) * 8 + z_lo * 4 + d["x"]


def exchange(v, axis, first):
    pairs = []
    for i in range(128):
        d = place(i)
        if axis == "core":
            d["core"] ^= 1
        elif (d["core"] == 0) == first:
            d[axis] ^= 1
        else:
            d[axis] = 3 - d[axis]
        pairs.append((i, number(d)))
    return lax.ppermute(v, AXES, pairs)


def half_of(axis, first):
    gx, gy = lax.axis_index("gx"), lax.axis_index("gy")
    core = gx % 2
    if axis == "core":
        return core
    p = {"x": gy % 4, "y": gx // 2 % 4, "z": gx // 8 * 2 + gy // 4}[axis]
    inner = ((p == 1) | (p == 2)).astype(jnp.int32)
    upper = (p >= 2).astype(jnp.int32)
    return jnp.where((core == 0) == first, inner, upper)


def add(a, b):
    return (a.astype(F32) + b.astype(F32)).astype(BF16)


def scatter_half(v, axis, first=True):
    n = v.shape[0] // 2
    b = half_of(axis, first)
    keep = lax.dynamic_slice_in_dim(v, b * n, n, 0)
    send = lax.dynamic_slice_in_dim(v, (1 - b) * n, n, 0)
    return add(keep, exchange(send, axis, first))


def gather_half(v, axis, first=True):
    b = half_of(axis, first)
    o = exchange(v, axis, first)
    return jnp.where(b == 0, jnp.concatenate([v, o], 0), jnp.concatenate([o, v], 0))


def total(parts, gate):
    order = [["core"] + ["xyz"[(k + s) % 3] for s in range(3)] for k in range(3)]
    parts = [scatter_half(p, "core") for p in parts]
    parts, gate = lax.optimization_barrier((parts, gate))
    for s in range(1, 4):
        parts = [scatter_half(p, o[s]) for p, o in zip(parts, order)]
    n = parts[0].shape[0]
    v = jnp.concatenate(parts, 0)
    v = scatter_half(v, "x", False)
    for axis in "yz":
        v = add(v, exchange(v, axis, False))
    v = gather_half(v, "x", False)
    parts = [v[n * k : n * k + n] for k in range(3)]
    for s in (3, 2, 1):
        parts = [gather_half(p, o[s]) for p, o in zip(parts, order)]
    return gate, parts, [exchange(p, "core", True) for p in parts]


def shift(v, d_gy, d_gx):
    pairs = []
    for gx in range(16):
        for gy in range(8):
            pairs.append((gx * 8 + gy, (gx + d_gx) % 16 * 8 + (gy + d_gy) % 8))
    return lax.ppermute(v, AXES, pairs)


def local(slide_tokens, tissue, grad_tokens, w_qkv, w_out):
    kb = jnp.broadcast_to(tissue.astype(BF16)[..., None], tissue.shape + (128,))
    up, down, left, corner = pack_call(slide_tokens, grad_tokens, kb)
    halo = (shift(up, -1, 0), shift(down, 1, 0), shift(left, 0, -1), shift(corner, 1, -1))
    mixed, dq, dk, dv, x, part = attn_call(slide_tokens, grad_tokens, kb, halo, w_qkv, w_out)
    attn, grad = finish_call(x, mixed, dq, dk, dv, w_qkv, w_out)
    (attn, grad), own, other = total([part[k] for k in range(3)], (attn, grad))

    up, down, side, corner = split_call(attn, grad)
    halo = (shift(up, -1, 0), shift(down, 1, 0), shift(side, 0, 1), shift(corner, -1, 1))
    block_out, grad_in = merge_call(slide_tokens, grad_tokens, attn, grad, halo)

    core = lax.axis_index("gx") % 2
    grad_wqkv, grad_wout = widen_call(core.astype(jnp.int32).reshape(1), own, other)
    return block_out, grad_in, grad_wqkv, grad_wout


def solution(mesh):
    tile = P("gy", "gx", None)
    return jax.shard_map(
        local,
        mesh=mesh,
        in_specs=(tile, P("gy", "gx"), tile, P(), P()),
        out_specs=(tile, tile, P(), P()),
        check_vma=False,
    )
```

```python
import functools
import math
import jax
import jax.numpy as jnp
from jax import lax
from jax.experimental import pallas as pl
from jax.experimental.pallas import tpu as pltpu
from jax.sharding import PartitionSpec as P

HEADS = 24
WIN = 8
SHIFT = 4
D = 768
GD = 256
EPS = 1e-05
SCALE = 1.0 / math.sqrt(32)
LOG2E = math.log2(math.e)
NT = (((1,), (1,)), ((), ()))
NN = (((1,), (0,)), ((), ()))
F32 = jnp.float32
BF16 = jnp.bfloat16


def mm(a, b, dims=NN):
    return lax.dot_general(a, b, dims, preferred_element_type=F32)


def spread(t, head_lane):
    zero = jnp.zeros_like(t)
    return jnp.concatenate([jnp.where(head_lane == h, t, zero) for h in range(4)], 0)


def gather_diag(full, head_lane):
    out = full[0:64]
    for h in range(1, 4):
        out = jnp.where(head_lane == h, full[64 * h : 64 * h + 64], out)
    return out


TOKENS = 1024
F = 2 * D + 128


def right_half(shape):
    return lax.broadcasted_iota(jnp.int32, shape, 1) >= 4


def seam(a, b):
    return jnp.where(right_half(a.shape), a, b)


def tile_of(t, j):
    return t[:, 8 * j : 8 * j + 8, :]


def pack_body(*refs):
    ins, (up, down, left, corner) = refs[:9], refs[9:]
    lane = 0
    for top, bottom, strip in (ins[0:3], ins[3:6], ins[6:9]):
        width = top.shape[-1]
        lanes = slice(lane, lane + width)
        lane += width
        for j in range(4):
            up[:, 8 * j : 8 * j + 8, lanes] = seam(tile_of(top, j), tile_of(top, j + 1))
        for j in range(3):
            down[:, 8 * j : 8 * j + 8, lanes] = seam(tile_of(bottom, j + 4), tile_of(bottom, j + 5))
        down[:, 24:32, lanes] = tile_of(bottom, 7)
        left[:, :, lanes] = strip[0:12]
        corner[:, :, lanes] = tile_of(bottom, 0)


def pack_call(x, g, kb):
    specs = []
    for t in (x, g, kb):
        w = t.shape[-1]
        specs += [
            pl.BlockSpec((4, 64, w), lambda i: (0, 0, 0)),
            pl.BlockSpec((4, 64, w), lambda i: (3, 0, 0)),
            pl.BlockSpec((16, 8, w), lambda i: (0, 0, 0)),
        ]
    shapes = [(4, 32, F), (4, 32, F), (12, 8, F), (4, 8, F)]
    return pl.pallas_call(
        pack_body,
        grid=(1,),
        in_specs=specs,
        out_specs=[pl.BlockSpec(sh, lambda i: (0, 0, 0)) for sh in shapes],
        out_shape=[jax.ShapeDtypeStruct(sh, BF16) for sh in shapes],
        compiler_params=pltpu.CompilerParams(vmem_limit_bytes=60 << 20),
        cost_estimate=pl.CostEstimate(flops=0, bytes_accessed=4_000_000, transcendentals=0),
        name="pack",
    )(x, x, x, g, g, g, kb, kb, kb)


def window_pieces(src, below, above, right, corner, lanes):
    out = []
    for j in range(8):
        nxt = tile_of(src[4:12], j + 1) if j < 7 else right[4:12, :, lanes]
        out.append(seam(tile_of(src[4:12], j), nxt))
    for j in range(4):
        own = seam(tile_of(src[12:16], j), tile_of(src[12:16], j + 1))
        out.append(jnp.concatenate([own, tile_of(below, j)[:, :, lanes]], 0))
    for j in range(4):
        nxt = tile_of(src[0:4], j + 5) if j < 3 else right[0:4, :, lanes]
        own = seam(tile_of(src[0:4], j + 4), nxt)
        top = tile_of(above, j)[:, :, lanes]
        if j == 3:
            top = seam(top, corner[:, :, lanes])
        out.append(jnp.concatenate([top, own], 0))
    return out


def attn_body(core_ref, x_ref, g_ref, kb_ref, below, above, right, corner, wq_ref, wk_ref, wv_ref, wo_ref,
              mixed_ref, dq_ref, dk_ref, dv_ref, xw, keep_ref, send_ref,
              gw, bias, hid, hid_t, qs, ks, vs, gm, mix_t):

    @pl.when(pl.program_id(0) == 0)
    def _():
        halo = (below, above, right, corner)
        for w, t in enumerate(window_pieces(x_ref, *halo, slice(0, D))):
            xw[64 * w : 64 * w + 64, :] = t.astype(F32).reshape(64, D).astype(BF16)
        for w, t in enumerate(window_pieces(g_ref, *halo, slice(D, 2 * D))):
            gw[64 * w : 64 * w + 64, :] = t.astype(F32).reshape(64, D).astype(BF16)
        lane = lax.broadcasted_iota(jnp.int32, (64, 128), 1) % 64
        itself = lane == lax.broadcasted_iota(jnp.int32, (64, 128), 0)
        for w, t in enumerate(window_pieces(kb_ref, *halo, slice(2 * D, F))):
            keep = t.astype(F32).reshape(64, 128) > 0.5
            bias[64 * w : 64 * w + 64, :] = jnp.where(keep | itself, 0.0, -1e30)

        @pl.loop(0, TOKENS // 128)
        def _(i):
            rows = pl.ds(pl.multiple_of(i * 128, 128), 128)
            x = xw[rows, :].astype(F32)
            c = x - jnp.mean(x, -1, keepdims=True)
            inv = lax.rsqrt(jnp.mean(c * c, -1, keepdims=True) + EPS)
            n = c * inv
            hid[rows, :] = n.astype(BF16)
            hid_t[:, rows] = jnp.transpose(n).astype(BF16)

    @pl.loop(0, 1)
    def _(i):
        rows = pl.ds(0, TOKENS)
        h = hid[rows, :]
        qs[rows, :] = mm(h, wq_ref[...]).astype(BF16)
        ks[rows, :] = mm(h, wk_ref[...]).astype(BF16)
        vs[rows, :] = mm(h, wv_ref[...]).astype(BF16)
        gm[rows, :] = mm(gw[rows, :], wo_ref[...], NT).astype(BF16)

    head_lane = lax.broadcasted_iota(jnp.int32, (64, 128), 1) // 32

    U = 4
    TN = (((0,), (0,)), ((), ()))

    @pl.loop(0, 16 // U)
    def _(w):
        keys = []
        for u in range(U):
            rows = pl.ds(pl.multiple_of(w * 64 * U + 64 * u, 64), 64)
            for s in range(GD // 128):
                keys.append((rows, slice(128 * s, 128 * s + 128)))
        ch = [(qs[c], ks[c], vs[c], gm[c]) for c in keys]
        allow = []
        for u in range(U):
            bb = bias[keys[2 * u][0], :]
            allow += [jnp.concatenate([bb, bb], 1)] * 2
        qb = [spread(c[0], head_lane) for c in ch]
        sc = [mm(c[1], b, NT) for c, b in zip(ch, qb)]
        gb = [spread(c[3], head_lane) for c in ch]
        dp = [mm(c[2], b, NT) for c, b in zip(ch, gb)]
        ps, pbs, dbs = [], [], []
        for s, b in zip(sc, allow):
            s = s * (SCALE * LOG2E) + b
            e = jnp.exp2(s - jnp.max(s, 0, keepdims=True))
            p = e * (1.0 / jnp.sum(e, 0, keepdims=True))
            ps.append(p)
            pbs.append(p.astype(BF16))
        for p, d in zip(ps, dp):
            ds = p * ((d - jnp.sum(d * p, 0, keepdims=True)) * SCALE)
            dbs.append(ds.astype(BF16))
        dv = [mm(p, b) for p, b in zip(pbs, gb)]
        mx = [mm(p, c[2], TN) for p, c in zip(pbs, ch)]
        dk = [mm(d, b) for d, b in zip(dbs, qb)]
        dq = [mm(d, c[1], TN) for d, c in zip(dbs, ch)]
        for i, c in enumerate(keys):
            dv_ref[c] = dv[i].astype(BF16)
            mixed_ref[c] = gather_diag(mx[i], head_lane).astype(BF16)
            dk_ref[c] = dk[i].astype(BF16)
            dq_ref[c] = gather_diag(dq[i], head_lane).astype(BF16)

    @pl.loop(0, TOKENS // 128)
    def _(i):
        rows = pl.ds(pl.multiple_of(i * 128, 128), 128)
        mix_t[:, rows] = jnp.transpose(mixed_ref[rows, :].astype(F32)).astype(BF16)

    core = core_ref[0]
    for out, half in ((keep_ref, core), (send_ref, 1 - core)):
        h = hid_t[pl.ds(pl.multiple_of(half * 384, 128), 384), :]
        out[0:384, 0:256] = mm(h, dq_ref[...]).astype(BF16)
        out[0:384, 256:512] = mm(h, dk_ref[...]).astype(BF16)
        out[0:384, 512:768] = mm(h, dv_ref[...]).astype(BF16)
        m = mix_t[pl.ds(pl.multiple_of(half * 128, 128), 128), :]
        out[384:512, :] = mm(m, gw[...]).astype(BF16)


def attn_call(core, x, g, kb, halo, w_qkv, w_out):
    fixed = lambda t: pl.BlockSpec(t.shape, lambda i, c: (0,) * t.ndim, pipeline_mode=pl.Buffered(1))
    cols = pl.BlockSpec((TOKENS, GD), lambda i, c: (0, i))
    wblock = lambda p: pl.BlockSpec((D, GD), lambda i, c: (0, 3 * p + i))
    half = pl.BlockSpec((512, D), lambda i, c: (i, 0))
    tok = jax.ShapeDtypeStruct((TOKENS, D), BF16)
    halves = jax.ShapeDtypeStruct((1536, D), BF16)
    return pl.pallas_call(
        attn_body,
        grid_spec=pltpu.PrefetchScalarGridSpec(
            num_scalar_prefetch=1,
            grid=(3,),
            in_specs=[fixed(t) for t in (x, g, kb, *halo)]
            + [wblock(0), wblock(1), wblock(2), pl.BlockSpec((GD, D), lambda i, c: (i, 0))],
            out_specs=[cols, cols, cols, cols, fixed(tok), half, half],
            scratch_shapes=[
                pltpu.VMEM((TOKENS, D), BF16),
                pltpu.VMEM((TOKENS, 128), F32),
                pltpu.VMEM((TOKENS, D), BF16),
                pltpu.VMEM((D, TOKENS), BF16),
                pltpu.VMEM((TOKENS, GD), BF16),
                pltpu.VMEM((TOKENS, GD), BF16),
                pltpu.VMEM((TOKENS, GD), BF16),
                pltpu.VMEM((TOKENS, GD), BF16),
                pltpu.VMEM((GD, TOKENS), BF16),
            ],
        ),
        out_shape=[tok, tok, tok, tok, tok, halves, halves],
        compiler_params=pltpu.CompilerParams(
            dimension_semantics=("arbitrary",), vmem_limit_bytes=48 << 20
        ),
        cost_estimate=pl.CostEstimate(
            flops=14_000_000_000, bytes_accessed=20_000_000, transcendentals=1_600_000
        ),
        name="attention",
    )(core, x, g, kb, *halo, w_qkv, w_qkv, w_qkv, w_out)


def finish_body(x_ref, mixed_ref, dq_ref, dk_ref, dv_ref, wqkv_ref, wo_ref, attn_ref, gs_ref):
    attn_ref[...] = mm(mixed_ref[...], wo_ref[...]).astype(BF16)
    dh = mm(dq_ref[...], wqkv_ref[:, 0:768], NT)
    dh += mm(dk_ref[...], wqkv_ref[:, 768:1536], NT)
    dh += mm(dv_ref[...], wqkv_ref[:, 1536:2304], NT)
    x = x_ref[...].astype(F32)
    c = x - jnp.mean(x, -1, keepdims=True)
    inv = lax.rsqrt(jnp.mean(c * c, -1, keepdims=True) + EPS)
    n = c * inv
    back = dh - jnp.mean(dh, -1, keepdims=True) - n * jnp.mean(dh * n, -1, keepdims=True)
    gs_ref[...] = (inv * back).astype(BF16)


def finish_call(x, mixed, dq, dk, dv, w_qkv, w_out):
    tokens = x.shape[0]
    tile = 512
    t = pl.BlockSpec((tile, D), lambda i: (i, 0))
    tok = jax.ShapeDtypeStruct((tokens, D), BF16)
    return pl.pallas_call(
        finish_body,
        grid=(tokens // tile,),
        in_specs=[t, t, t, t, t,
                  pl.BlockSpec((D, 3 * D), lambda i: (0, 0), pipeline_mode=pl.Buffered(1)),
                  pl.BlockSpec((D, D), lambda i: (0, 0), pipeline_mode=pl.Buffered(1))],
        out_specs=[t, t],
        out_shape=[tok, tok],
        compiler_params=pltpu.CompilerParams(
            dimension_semantics=("arbitrary",), vmem_limit_bytes=60 << 20
        ),
        cost_estimate=pl.CostEstimate(
            flops=4_800_000_000, bytes_accessed=16_000_000, transcendentals=0
        ),
        name="finish",
    )(x, mixed, dq, dk, dv, w_qkv, w_out)


def merge_body(x_ref, g_ref, attn_ref, grad_ref, below, above, left, corner, out_ref, gin_ref):
    for src, win, dst, lanes in (
        (x_ref, attn_ref, out_ref, slice(0, D)),
        (g_ref, grad_ref, gin_ref, slice(D, 2 * D)),
    ):
        piece = lambda w: win[64 * w : 64 * w + 64, :].astype(F32).reshape(8, 8, D)
        far = lambda t, j: tile_of(t, j)[:, :, lanes].astype(F32)
        mids = [left[4:12, :, lanes].astype(F32)] + [piece(j) for j in range(8)]
        lows = [corner[:, :, lanes].astype(F32)] + [piece(8 + j)[0:4] for j in range(4)] + [far(below, j) for j in range(4)]
        tops = [left[0:4, :, lanes].astype(F32)] + [far(above, j) for j in range(4)] + [piece(12 + j)[4:8] for j in range(4)]
        for j in range(8):
            cols = slice(8 * j, 8 * j + 8)
            for rows, t in ((slice(4, 12), mids), (slice(12, 16), lows), (slice(0, 4), tops)):
                add = seam(t[j + 1], t[j])
                dst[rows, cols, :] = (src[rows, cols, :].astype(F32) + add).astype(BF16)


def merge_call(x, g, attn, grad, halo):
    tile = jax.ShapeDtypeStruct(x.shape, BF16)
    return pl.pallas_call(
        merge_body,
        out_shape=[tile, tile],
        compiler_params=pltpu.CompilerParams(vmem_limit_bytes=32 << 20),
        cost_estimate=pl.CostEstimate(flops=3_000_000, bytes_accessed=11_000_000, transcendentals=0),
        name="merge",
    )(x, g, attn, grad, *halo)


def split_body(attn_ref, grad_ref, up, down, side, corner):
    for win, lanes in ((attn_ref, slice(0, D)), (grad_ref, slice(D, 2 * D))):
        piece = lambda w: win[64 * w : 64 * w + 64, :].astype(F32).reshape(8, 8, D).astype(BF16)
        for j in range(4):
            cols = slice(8 * j, 8 * j + 8)
            up[:, cols, lanes] = piece(12 + j)[0:4]
            down[:, cols, lanes] = piece(8 + j)[4:8]
        side[0:4, :, lanes] = piece(15)[4:8]
        side[4:12, :, lanes] = piece(7)
        corner[:, :, lanes] = piece(15)[0:4]


def split_call(attn, grad):
    shapes = [(4, 32, 2 * D), (4, 32, 2 * D), (12, 8, 2 * D), (4, 8, 2 * D)]
    return pl.pallas_call(
        split_body,
        out_shape=[jax.ShapeDtypeStruct(sh, BF16) for sh in shapes],
        compiler_params=pltpu.CompilerParams(vmem_limit_bytes=16 << 20),
        cost_estimate=pl.CostEstimate(flops=0, bytes_accessed=5_000_000, transcendentals=0),
        name="split",
    )(attn, grad)


def combine_body(bits, keep, recv, *outs):
    for k in range(3):
        for out, half in ((outs[k], bits[k]), (outs[3 + k], 1 - bits[k])):
            rows = pl.ds(pl.multiple_of(512 * k + half * 256, 256), 256)
            out[...] = (keep[rows, :].astype(F32) + recv[rows, :].astype(F32)).astype(BF16)


def combine_call(bits, keep, recv):
    whole = pl.BlockSpec((1536, D), lambda i, c: (0, 0), pipeline_mode=pl.Buffered(1))
    half = pl.BlockSpec((256, D), lambda i, c: (0, 0), pipeline_mode=pl.Buffered(1))
    return pl.pallas_call(
        combine_body,
        grid_spec=pltpu.PrefetchScalarGridSpec(
            num_scalar_prefetch=1, grid=(1,), in_specs=[whole] * 2, out_specs=[half] * 6
        ),
        out_shape=[jax.ShapeDtypeStruct((256, D), BF16)] * 6,
        compiler_params=pltpu.CompilerParams(vmem_limit_bytes=16 << 20),
        cost_estimate=pl.CostEstimate(flops=1_200_000, bytes_accessed=7_000_000, transcendentals=0),
        name="combine",
    )(bits, keep, recv)


def widen_body(core_ref, own, other, wqkv, wout):
    j = pl.program_id(0)
    core = core_ref[0]

    def put(src):
        for k in range(3):
            rows = pl.ds(pl.multiple_of(512 * k + j % 3 * 128, 128), 128)
            for p in range(3):
                wqkv[:, D * p + GD * k : D * p + GD * k + GD] = src[rows, GD * p : GD * p + GD].astype(F32)

    @pl.when((j < 6) & (j // 3 == core))
    def _():
        put(own)

    @pl.when((j < 6) & (j // 3 != core))
    def _():
        put(other)

    @pl.when(j == 6)
    def _():
        for src, half in ((own, core), (other, 1 - core)):
            for k in range(3):
                rows = pl.ds(pl.multiple_of(GD * k + half * 128, 128), 128)
                wout[rows, :] = src[512 * k + 384 : 512 * k + 512, :].astype(F32)


def widen_call(core, own, other):
    half = pl.BlockSpec((1536, D), lambda j, c: (0, 0), pipeline_mode=pl.Buffered(1))
    return pl.pallas_call(
        widen_body,
        grid_spec=pltpu.PrefetchScalarGridSpec(
            num_scalar_prefetch=1,
            grid=(7,),
            in_specs=[half] * 2,
            out_specs=[
                pl.BlockSpec((128, 3 * D), lambda j, c: (jnp.minimum(j, 5), 0)),
                pl.BlockSpec((D, D), lambda j, c: (0, 0)),
            ],
        ),
        out_shape=[jax.ShapeDtypeStruct((D, 3 * D), F32), jax.ShapeDtypeStruct((D, D), F32)],
        compiler_params=pltpu.CompilerParams(
            dimension_semantics=("arbitrary",), vmem_limit_bytes=32 << 20
        ),
        cost_estimate=pl.CostEstimate(flops=0, bytes_accessed=14_000_000, transcendentals=0),
        name="widen",
    )(core, own, other)


AXES = ("gx", "gy")


def place(i):
    gx, gy = divmod(i, 8)
    z_hi, y, core = gx // 8, gx // 2 % 4, gx % 2
    z_lo, x = divmod(gy, 4)
    return {"core": core, "x": x, "y": y, "z": 2 * z_hi + z_lo}


def number(d):
    z_hi, z_lo = divmod(d["z"], 2)
    return ((z_hi * 4 + d["y"]) * 2 + d["core"]) * 8 + z_lo * 4 + d["x"]


def exchange(v, axis, first):
    pairs = []
    for i in range(128):
        d = place(i)
        if axis == "core":
            d["core"] ^= 1
        elif (d["core"] == 0) == first:
            d[axis] ^= 1
        else:
            d[axis] = 3 - d[axis]
        pairs.append((i, number(d)))
    return lax.ppermute(v, AXES, pairs)


def half_of(axis, first):
    gx, gy = lax.axis_index("gx"), lax.axis_index("gy")
    core = gx % 2
    if axis == "core":
        return core
    p = {"x": gy % 4, "y": gx // 2 % 4, "z": gx // 8 * 2 + gy // 4}[axis]
    inner = ((p == 1) | (p == 2)).astype(jnp.int32)
    upper = (p >= 2).astype(jnp.int32)
    return jnp.where((core == 0) == first, inner, upper)


def add(a, b):
    return (a.astype(F32) + b.astype(F32)).astype(BF16)


def scatter_half(v, axis, first=True):
    n = v.shape[0] // 2
    b = half_of(axis, first)
    keep = lax.dynamic_slice_in_dim(v, b * n, n, 0)
    send = lax.dynamic_slice_in_dim(v, (1 - b) * n, n, 0)
    return add(keep, exchange(send, axis, first))


def gather_half(v, axis, first=True):
    b = half_of(axis, first)
    o = exchange(v, axis, first)
    return jnp.where(b == 0, jnp.concatenate([v, o], 0), jnp.concatenate([o, v], 0))


def total(keep, send, gate):
    axes = [["xyz"[(k + s) % 3] for s in range(3)] for k in range(3)]
    recv = exchange(send, "core", True)
    keep, recv, gate = lax.optimization_barrier((keep, recv, gate))
    bits = jnp.stack([half_of(a[0], True) for a in axes]).astype(jnp.int32)
    halves = combine_call(bits, keep, recv)
    parts = [add(halves[k], exchange(halves[3 + k], a[0], True)) for k, a in enumerate(axes)]
    parts = [scatter_half(p, a[1]) for p, a in zip(parts, axes)]
    for axis, first in ((2, True), (0, False), (1, False), (2, False)):
        parts = [add(p, exchange(p, a[axis], first)) for p, a in zip(parts, axes)]
    for s in (1, 0):
        parts = [gather_half(p, a[s]) for p, a in zip(parts, axes)]
    return jnp.concatenate(parts, 0), gate


def shift(v, d_gy, d_gx):
    pairs = []
    for gx in range(16):
        for gy in range(8):
            pairs.append((gx * 8 + gy, (gx + d_gx) % 16 * 8 + (gy + d_gy) % 8))
    return lax.ppermute(v, AXES, pairs)


def local(slide_tokens, tissue, grad_tokens, w_qkv, w_out):
    kb = jnp.broadcast_to(tissue.astype(BF16)[..., None], tissue.shape + (128,))
    core = (lax.axis_index("gx") % 2).astype(jnp.int32).reshape(1)
    up, down, left, corner = pack_call(slide_tokens, grad_tokens, kb)
    corner = shift(corner, 1, -1)
    left = shift(left, 0, -1)
    halo = (shift(up, -1, 0), shift(down, 1, 0), left, corner)
    mixed, dq, dk, dv, x, keep, send = attn_call(core, slide_tokens, grad_tokens, kb, halo, w_qkv, w_out)
    attn, grad = finish_call(x, mixed, dq, dk, dv, w_qkv, w_out)
    own, (attn, grad) = total(keep, send, (attn, grad))

    own, borders = lax.optimization_barrier((own, tuple(split_call(attn, grad))))
    up, down, side, corner = borders
    corner = shift(corner, -1, 1)
    side = shift(side, 0, 1)
    halo = (shift(up, -1, 0), shift(down, 1, 0), side, corner)
    grads = widen_call(core, own, exchange(own, "core", True))
    halo, grads = lax.optimization_barrier((halo, tuple(grads)))
    block_out, grad_in = merge_call(slide_tokens, grad_tokens, attn, grad, halo)
    return block_out, grad_in, *grads


def solution(mesh):
    tile = P("gy", "gx", None)
    return jax.shard_map(
        local,
        mesh=mesh,
        in_specs=(tile, P("gy", "gx"), tile, P(), P()),
        out_specs=(tile, tile, P(), P()),
        check_vma=False,
    )
```

```python
import functools
import math
import jax
import jax.numpy as jnp
from jax import lax
from jax.experimental import pallas as pl
from jax.experimental.pallas import tpu as pltpu
from jax.sharding import PartitionSpec as P

HEADS = 24
WIN = 8
SHIFT = 4
D = 768
GD = 256
EPS = 1e-05
SCALE = 1.0 / math.sqrt(32)
LOG2E = math.log2(math.e)
NT = (((1,), (1,)), ((), ()))
NN = (((1,), (0,)), ((), ()))
F32 = jnp.float32
BF16 = jnp.bfloat16


def mm(a, b, dims=NN):
    return lax.dot_general(a, b, dims, preferred_element_type=F32)


def spread(t, head_lane):
    zero = jnp.zeros_like(t)
    return jnp.concatenate([jnp.where(head_lane == h, t, zero) for h in range(4)], 0)


def gather_diag(full, head_lane):
    out = full[0:64]
    for h in range(1, 4):
        out = jnp.where(head_lane == h, full[64 * h : 64 * h + 64], out)
    return out


TOKENS = 1024
HERE = pl.BlockSpec(memory_space=pltpu.VMEM)
F = 2 * D + 128


def right_half(shape):
    return lax.broadcasted_iota(jnp.int32, shape, 1) >= 4


def seam(a, b):
    return jnp.where(right_half(a.shape), a, b)


def tile_of(t, j):
    return t[:, 8 * j : 8 * j + 8, :]


def pack_body(*refs):
    ins, (up, down, left, corner) = refs[:9], refs[9:]
    lane = 0
    for top, bottom, strip in (ins[0:3], ins[3:6], ins[6:9]):
        width = top.shape[-1]
        lanes = slice(lane, lane + width)
        lane += width
        for j in range(4):
            up[:, 8 * j : 8 * j + 8, lanes] = seam(tile_of(top, j), tile_of(top, j + 1))
        for j in range(3):
            down[:, 8 * j : 8 * j + 8, lanes] = seam(tile_of(bottom, j + 4), tile_of(bottom, j + 5))
        down[:, 24:32, lanes] = tile_of(bottom, 7)
        left[:, :, lanes] = strip[0:12]
        corner[:, :, lanes] = tile_of(bottom, 0)


def pack_call(x, g, kb):
    specs = []
    for t in (x, g, kb):
        w = t.shape[-1]
        specs += [
            pl.BlockSpec((4, 64, w), lambda i: (0, 0, 0)),
            pl.BlockSpec((4, 64, w), lambda i: (3, 0, 0)),
            pl.BlockSpec((16, 8, w), lambda i: (0, 0, 0)),
        ]
    shapes = [(4, 32, F), (4, 32, F), (12, 8, F), (4, 8, F)]
    return pl.pallas_call(
        pack_body,
        grid=(1,),
        in_specs=specs,
        out_specs=[pl.BlockSpec(sh, lambda i: (0, 0, 0)) for sh in shapes],
        out_shape=[jax.ShapeDtypeStruct(sh, BF16) for sh in shapes],
        compiler_params=pltpu.CompilerParams(vmem_limit_bytes=60 << 20),
        cost_estimate=pl.CostEstimate(flops=0, bytes_accessed=4_000_000, transcendentals=0),
        name="pack",
    )(x, x, x, g, g, g, kb, kb, kb)


def window_pieces(src, below, above, right, corner, lanes):
    out = []
    for j in range(8):
        nxt = tile_of(src[4:12], j + 1) if j < 7 else right[4:12, :, lanes]
        out.append(seam(tile_of(src[4:12], j), nxt))
    for j in range(4):
        own = seam(tile_of(src[12:16], j), tile_of(src[12:16], j + 1))
        out.append(jnp.concatenate([own, tile_of(below, j)[:, :, lanes]], 0))
    for j in range(4):
        nxt = tile_of(src[0:4], j + 5) if j < 3 else right[0:4, :, lanes]
        own = seam(tile_of(src[0:4], j + 4), nxt)
        top = tile_of(above, j)[:, :, lanes]
        if j == 3:
            top = seam(top, corner[:, :, lanes])
        out.append(jnp.concatenate([top, own], 0))
    return out


def attn_body(core_ref, x_ref, g_ref, kb_ref, corner, right, below, above, wq_ref, wk_ref, wv_ref, wg_ref, wqkv_hbm, wo_hbm,
              attn_ref, gs_ref, up, down, side, edge, keep_ref, send_ref,
              mixed_ref, dq_ref, dk_ref, dv_ref, xw, wqkv, wo, sems, gw, bias, hid, hid_t, qs, ks, vs, gm, mix_t):

    loads = [
        pltpu.make_async_copy(wqkv_hbm, wqkv, sems.at[0]),
        pltpu.make_async_copy(wo_hbm, wo, sems.at[1]),
    ]

    @pl.when(pl.program_id(0) == 0)
    def _():
        for load in loads:
            load.start()
        halo = (below, above, right, corner)
        for w, t in enumerate(window_pieces(x_ref, *halo, slice(0, D))):
            xw[64 * w : 64 * w + 64, :] = t.astype(F32).reshape(64, D).astype(BF16)
        for w, t in enumerate(window_pieces(g_ref, *halo, slice(D, 2 * D))):
            gw[64 * w : 64 * w + 64, :] = t.astype(F32).reshape(64, D).astype(BF16)
        lane = lax.broadcasted_iota(jnp.int32, (64, 128), 1) % 64
        itself = lane == lax.broadcasted_iota(jnp.int32, (64, 128), 0)
        for w, t in enumerate(window_pieces(kb_ref, *halo, slice(2 * D, F))):
            keep = t.astype(F32).reshape(64, 128) > 0.5
            bias[64 * w : 64 * w + 64, :] = jnp.where(keep | itself, 0.0, -1e30)

        @pl.loop(0, TOKENS // 128)
        def _(i):
            rows = pl.ds(pl.multiple_of(i * 128, 128), 128)
            x = xw[rows, :].astype(F32)
            c = x - jnp.mean(x, -1, keepdims=True)
            inv = lax.rsqrt(jnp.mean(c * c, -1, keepdims=True) + EPS)
            n = c * inv
            hid[rows, :] = n.astype(BF16)
            hid_t[:, rows] = jnp.transpose(n).astype(BF16)

    group = pl.program_id(0)
    base = pl.multiple_of(group * GD, GD)
    cols = pl.ds(base, GD)
    h = hid[...]
    for w, out in ((wq_ref, qs), (wk_ref, ks), (wv_ref, vs)):
        out[...] = mm(h, w[...]).astype(BF16)
    gm[...] = mm(gw[...], wg_ref[...], NT).astype(BF16)

    head_lane = lax.broadcasted_iota(jnp.int32, (64, 128), 1) // 32

    U = 4
    TN = (((0,), (0,)), ((), ()))

    @pl.loop(0, 16 // U)
    def _(w):
        keys = []
        for u in range(U):
            rows = pl.ds(pl.multiple_of(w * 64 * U + 64 * u, 64), 64)
            for s in range(GD // 128):
                keys.append((rows, slice(128 * s, 128 * s + 128)))
        ch = [(qs[c], ks[c], vs[c], gm[c]) for c in keys]
        allow = []
        for u in range(U):
            bb = bias[keys[2 * u][0], :]
            allow += [jnp.concatenate([bb, bb], 1)] * 2
        qb = [spread(c[0], head_lane) for c in ch]
        sc = [mm(c[1], b, NT) for c, b in zip(ch, qb)]
        gb = [spread(c[3], head_lane) for c in ch]
        dp = [mm(c[2], b, NT) for c, b in zip(ch, gb)]
        ps, pbs, dbs = [], [], []
        for s, b in zip(sc, allow):
            s = s * (SCALE * LOG2E) + b
            e = jnp.exp2(s - jnp.max(s, 0, keepdims=True))
            p = e * (1.0 / jnp.sum(e, 0, keepdims=True))
            ps.append(p)
            pbs.append(p.astype(BF16))
        for p, d in zip(ps, dp):
            ds = p * ((d - jnp.sum(d * p, 0, keepdims=True)) * SCALE)
            dbs.append(ds.astype(BF16))
        dv = [mm(p, b) for p, b in zip(pbs, gb)]
        mx = [mm(p, c[2], TN) for p, c in zip(pbs, ch)]
        dk = [mm(d, b) for d, b in zip(dbs, qb)]
        dq = [mm(d, c[1], TN) for d, c in zip(dbs, ch)]
        for i, (rows, lanes) in enumerate(keys):
            c = rows, pl.ds(pl.multiple_of(base + lanes.start, 128), 128)
            dv_ref[c] = dv[i].astype(BF16)
            mixed_ref[c] = gather_diag(mx[i], head_lane).astype(BF16)
            dk_ref[c] = dk[i].astype(BF16)
            dq_ref[c] = gather_diag(dq[i], head_lane).astype(BF16)

    @pl.loop(0, TOKENS // 128)
    def _(i):
        rows = pl.ds(pl.multiple_of(i * 128, 128), 128)
        mix_t[:, rows] = jnp.transpose(mixed_ref[rows, cols].astype(F32)).astype(BF16)

    core = core_ref[0]
    for out, half in ((keep_ref, core), (send_ref, 1 - core)):
        h = hid_t[pl.ds(pl.multiple_of(half * 384, 128), 384), :]
        for p, t in enumerate((dq_ref, dk_ref, dv_ref)):
            out[0:384, GD * p : GD * p + GD] = mm(h, t[:, cols]).astype(BF16)
        m = mix_t[pl.ds(pl.multiple_of(half * 128, 128), 128), :]
        out[384:512, :] = mm(m, gw[...]).astype(BF16)

    @pl.when(group == 2)
    def _():
        for load in loads:
            load.wait()

        @pl.loop(0, 2)
        def _(i):
            rows = pl.ds(pl.multiple_of(i * 512, 512), 512)
            attn_ref[rows, :] = mm(mixed_ref[rows, :], wo[...]).astype(BF16)
            dh = mm(dq_ref[rows, :], wqkv[:, 0:768], NT)
            dh += mm(dk_ref[rows, :], wqkv[:, 768:1536], NT)
            dh += mm(dv_ref[rows, :], wqkv[:, 1536:2304], NT)
            x = xw[rows, :].astype(F32)
            c = x - jnp.mean(x, -1, keepdims=True)
            inv = lax.rsqrt(jnp.mean(c * c, -1, keepdims=True) + EPS)
            n = c * inv
            back = dh - jnp.mean(dh, -1, keepdims=True) - n * jnp.mean(dh * n, -1, keepdims=True)
            gs_ref[rows, :] = (inv * back).astype(BF16)

        for win, lanes in ((attn_ref, slice(0, D)), (gs_ref, slice(D, 2 * D))):
            piece = lambda w: win[64 * w : 64 * w + 64, :].astype(F32).reshape(8, 8, D).astype(BF16)
            for j in range(4):
                at = slice(8 * j, 8 * j + 8)
                up[:, at, lanes] = piece(12 + j)[0:4]
                down[:, at, lanes] = piece(8 + j)[4:8]
            side[0:4, :, lanes] = piece(15)[4:8]
            side[4:12, :, lanes] = piece(7)
            edge[:, :, lanes] = piece(15)[0:4]


def attn_call(core, x, g, kb, halo, w_qkv, w_out):
    fixed = lambda t: pl.BlockSpec(t.shape, lambda i, c: (0,) * len(t.shape), pipeline_mode=pl.Buffered(1))
    wblock = lambda p: pl.BlockSpec((D, GD), lambda i, c: (0, 3 * p + i))
    half = pl.BlockSpec((512, D), lambda i, c: (i, 0))
    far = pl.BlockSpec(memory_space=pl.ANY)
    tok = jax.ShapeDtypeStruct((TOKENS, D), BF16)
    halves = jax.ShapeDtypeStruct((1536, D), BF16)
    borders = [jax.ShapeDtypeStruct((r, c, 2 * D), BF16) for r, c in ((4, 32), (4, 32), (12, 8), (4, 8))]
    return pl.pallas_call(
        attn_body,
        grid_spec=pltpu.PrefetchScalarGridSpec(
            num_scalar_prefetch=1,
            grid=(3,),
            in_specs=[fixed(t) for t in (x, g, kb, *halo)]
            + [wblock(0), wblock(1), wblock(2), pl.BlockSpec((GD, D), lambda i, c: (i, 0)), far, far],
            out_specs=[fixed(t) for t in (tok, tok, *borders)] + [half, half],
            scratch_shapes=[pltpu.VMEM((TOKENS, D), BF16)] * 5
            + [
                pltpu.VMEM((D, 3 * D), BF16),
                pltpu.VMEM((D, D), BF16),
                pltpu.SemaphoreType.DMA((2,)),
                pltpu.VMEM((TOKENS, D), BF16),
                pltpu.VMEM((TOKENS, 128), F32),
                pltpu.VMEM((TOKENS, D), BF16),
                pltpu.VMEM((D, TOKENS), BF16),
                pltpu.VMEM((TOKENS, GD), BF16),
                pltpu.VMEM((TOKENS, GD), BF16),
                pltpu.VMEM((TOKENS, GD), BF16),
                pltpu.VMEM((TOKENS, GD), BF16),
                pltpu.VMEM((GD, TOKENS), BF16),
            ],
        ),
        out_shape=[tok, tok, *borders, halves, halves],
        compiler_params=pltpu.CompilerParams(
            dimension_semantics=("arbitrary",), vmem_limit_bytes=56 << 20
        ),
        cost_estimate=pl.CostEstimate(
            flops=16_000_000_000, bytes_accessed=25_000_000, transcendentals=1_600_000
        ),
        name="attention",
    )(core, x, g, kb, *halo, w_qkv, w_qkv, w_qkv, w_out, w_qkv, w_out)


def merge_body(x_ref, g_ref, attn_ref, grad_ref, corner, left, below, above, out_ref, gin_ref):
    for src, win, dst, lanes in (
        (x_ref, attn_ref, out_ref, slice(0, D)),
        (g_ref, grad_ref, gin_ref, slice(D, 2 * D)),
    ):
        piece = lambda w: win[64 * w : 64 * w + 64, :].astype(F32).reshape(8, 8, D)
        far = lambda t, j: tile_of(t, j)[:, :, lanes].astype(F32)
        mids = [left[4:12, :, lanes].astype(F32)] + [piece(j) for j in range(8)]
        lows = [corner[:, :, lanes].astype(F32)] + [piece(8 + j)[0:4] for j in range(4)] + [far(below, j) for j in range(4)]
        tops = [left[0:4, :, lanes].astype(F32)] + [far(above, j) for j in range(4)] + [piece(12 + j)[4:8] for j in range(4)]
        for j in range(8):
            cols = slice(8 * j, 8 * j + 8)
            for rows, t in ((slice(4, 12), mids), (slice(12, 16), lows), (slice(0, 4), tops)):
                add = seam(t[j + 1], t[j])
                dst[rows, cols, :] = (src[rows, cols, :].astype(F32) + add).astype(BF16)


def merge_call(x, g, attn, grad, halo):
    tile = jax.ShapeDtypeStruct(x.shape, BF16)
    return pl.pallas_call(
        merge_body,
        out_shape=[tile, tile],
        compiler_params=pltpu.CompilerParams(vmem_limit_bytes=32 << 20),
        cost_estimate=pl.CostEstimate(flops=3_000_000, bytes_accessed=11_000_000, transcendentals=0),
        name="merge",
    )(x, g, attn, grad, *halo)


def combine_body(bits, keep, recv, *outs):
    for k in range(3):

        @pl.when(pl.program_id(0) == k)
        def _():
            for out, half in ((outs[k], bits[k]), (outs[3 + k], 1 - bits[k])):
                rows = pl.ds(pl.multiple_of(half * 256, 256), 256)
                out[...] = (keep[rows, :].astype(F32) + recv[rows, :].astype(F32)).astype(BF16)


def combine_call(bits, keep, recv):
    part = pl.BlockSpec((512, D), lambda i, c: (i, 0))
    half = pl.BlockSpec((256, D), lambda i, c: (0, 0), pipeline_mode=pl.Buffered(1))
    return pl.pallas_call(
        combine_body,
        grid_spec=pltpu.PrefetchScalarGridSpec(
            num_scalar_prefetch=1, grid=(3,), in_specs=[part] * 2, out_specs=[half] * 6
        ),
        out_shape=[jax.ShapeDtypeStruct((256, D), BF16)] * 6,
        compiler_params=pltpu.CompilerParams(
            dimension_semantics=("arbitrary",), vmem_limit_bytes=16 << 20
        ),
        cost_estimate=pl.CostEstimate(flops=1_200_000, bytes_accessed=7_000_000, transcendentals=0),
        name="combine",
    )(bits, keep, recv)


def join_body(bits, *refs):
    out = refs[-1]
    n = refs[0].shape[0]
    for k in range(len(refs) // 2):
        out[pl.ds(pl.multiple_of(n * (2 * k + bits[k]), n), n), :] = refs[2 * k][...]
        out[pl.ds(pl.multiple_of(n * (2 * k + 1 - bits[k]), n), n), :] = refs[2 * k + 1][...]


def join_call(bits, *halves):
    rows = len(halves) * halves[0].shape[0]
    return pl.pallas_call(
        join_body,
        grid_spec=pltpu.PrefetchScalarGridSpec(
            num_scalar_prefetch=1, grid=(1,), in_specs=[HERE] * len(halves), out_specs=HERE
        ),
        out_shape=jax.ShapeDtypeStruct((rows, D), BF16),
        compiler_params=pltpu.CompilerParams(vmem_limit_bytes=16 << 20),
        cost_estimate=pl.CostEstimate(flops=0, bytes_accessed=3072 * rows, transcendentals=0),
        name="join",
    )(bits, *halves)


def widen_body(core_ref, own, other, wqkv, wout):
    j = pl.program_id(0)
    core = core_ref[0]

    def put(src):
        for k in range(3):
            rows = pl.ds(pl.multiple_of(512 * k + j % 3 * 128, 128), 128)
            for p in range(3):
                wqkv[:, D * p + GD * k : D * p + GD * k + GD] = src[rows, GD * p : GD * p + GD].astype(F32)

    @pl.when((j < 6) & (j // 3 == core))
    def _():
        put(own)

    @pl.when((j < 6) & (j // 3 != core))
    def _():
        put(other)

    @pl.when(j == 6)
    def _():
        for src, half in ((own, core), (other, 1 - core)):
            for k in range(3):
                rows = pl.ds(pl.multiple_of(GD * k + half * 128, 128), 128)
                wout[rows, :] = src[512 * k + 384 : 512 * k + 512, :].astype(F32)


def widen_call(core, own, other):
    return pl.pallas_call(
        widen_body,
        grid_spec=pltpu.PrefetchScalarGridSpec(
            num_scalar_prefetch=1,
            grid=(7,),
            in_specs=[HERE] * 2,
            out_specs=[
                pl.BlockSpec((128, 3 * D), lambda j, c: (jnp.minimum(j, 5), 0)),
                pl.BlockSpec((D, D), lambda j, c: (0, 0)),
            ],
        ),
        out_shape=[jax.ShapeDtypeStruct((D, 3 * D), F32), jax.ShapeDtypeStruct((D, D), F32)],
        compiler_params=pltpu.CompilerParams(
            dimension_semantics=("arbitrary",), vmem_limit_bytes=32 << 20
        ),
        cost_estimate=pl.CostEstimate(flops=0, bytes_accessed=14_000_000, transcendentals=0),
        name="widen",
    )(core, own, other)


AXES = ("gx", "gy")


def place(i):
    gx, gy = divmod(i, 8)
    z_hi, y, core = gx // 8, gx // 2 % 4, gx % 2
    z_lo, x = divmod(gy, 4)
    return {"core": core, "x": x, "y": y, "z": 2 * z_hi + z_lo}


def number(d):
    z_hi, z_lo = divmod(d["z"], 2)
    return ((z_hi * 4 + d["y"]) * 2 + d["core"]) * 8 + z_lo * 4 + d["x"]


def exchange(v, axis, first):
    pairs = []
    for i in range(128):
        d = place(i)
        if axis == "core":
            d["core"] ^= 1
        elif (d["core"] == 0) == first:
            d[axis] ^= 1
        else:
            d[axis] = 3 - d[axis]
        pairs.append((i, number(d)))
    return lax.ppermute(v, AXES, pairs)


def half_of(axis, first):
    gx, gy = lax.axis_index("gx"), lax.axis_index("gy")
    core = gx % 2
    if axis == "core":
        return core
    p = {"x": gy % 4, "y": gx // 2 % 4, "z": gx // 8 * 2 + gy // 4}[axis]
    inner = ((p == 1) | (p == 2)).astype(jnp.int32)
    upper = (p >= 2).astype(jnp.int32)
    return jnp.where((core == 0) == first, inner, upper)


def add(a, b):
    return (a.astype(F32) + b.astype(F32)).astype(BF16)


def scatter_half(v, axis, first=True):
    n = v.shape[0] // 2
    b = half_of(axis, first)
    keep = lax.dynamic_slice_in_dim(v, b * n, n, 0)
    send = lax.dynamic_slice_in_dim(v, (1 - b) * n, n, 0)
    return add(keep, exchange(send, axis, first))


def total(keep, send):
    axes = [["xyz"[(k + s) % 3] for s in range(3)] for k in range(3)]
    recv = exchange(send, "core", True)
    bits = jnp.stack([half_of(a[0], True) for a in axes]).astype(jnp.int32)
    halves = combine_call(bits, keep, recv)
    parts = [add(halves[k], exchange(halves[3 + k], a[0], True)) for k, a in enumerate(axes)]
    parts = [scatter_half(p, a[1]) for p, a in zip(parts, axes)]
    for axis, first in ((2, True), (0, False), (1, False), (2, False)):
        parts = [add(p, exchange(p, a[axis], first)) for p, a in zip(parts, axes)]
    second = [half_of(a[1], True).astype(jnp.int32).reshape(1) for a in axes]
    parts = [join_call(b, p, exchange(p, a[1], True)) for b, p, a in zip(second, parts, axes)]
    halves = []
    for p, a in zip(parts, axes):
        halves += [p, exchange(p, a[0], True)]
    return join_call(bits, *halves)


def shift(v, d_gy, d_gx):
    pairs = []
    for gx in range(16):
        for gy in range(8):
            pairs.append((gx * 8 + gy, (gx + d_gx) % 16 * 8 + (gy + d_gy) % 8))
    return lax.ppermute(v, AXES, pairs)


def local(slide_tokens, tissue, grad_tokens, w_qkv, w_out):
    kb = jnp.broadcast_to(tissue.astype(BF16)[..., None], tissue.shape + (128,))
    core = (lax.axis_index("gx") % 2).astype(jnp.int32).reshape(1)
    up, down, left, corner = pack_call(slide_tokens, grad_tokens, kb)
    halo = (shift(corner, 1, -1), shift(left, 0, -1), shift(up, -1, 0), shift(down, 1, 0))
    attn, grad, up, down, side, edge, keep, send = attn_call(
        core, slide_tokens, grad_tokens, kb, halo, w_qkv, w_out
    )
    own = total(keep, send)

    own, (up, down, side, edge) = lax.optimization_barrier((own, (up, down, side, edge)))
    halo = (shift(edge, -1, 1), shift(side, 0, 1), shift(up, -1, 0), shift(down, 1, 0))
    grads = widen_call(core, own, exchange(own, "core", True))
    halo, grads = lax.optimization_barrier((halo, tuple(grads)))
    block_out, grad_in = merge_call(slide_tokens, grad_tokens, attn, grad, halo)
    return block_out, grad_in, *grads


def solution(mesh):
    tile = P("gy", "gx", None)
    return jax.shard_map(
        local,
        mesh=mesh,
        in_specs=(tile, P("gy", "gx"), tile, P(), P()),
        out_specs=(tile, tile, P(), P()),
        check_vma=False,
    )
```

```python
import functools
import math
import jax
import jax.numpy as jnp
from jax import lax
from jax.experimental import pallas as pl
from jax.experimental.pallas import tpu as pltpu
from jax.sharding import PartitionSpec as P

HEADS = 24
WIN = 8
SHIFT = 4
D = 768
GD = 256
EPS = 1e-05
SCALE = 1.0 / math.sqrt(32)
LOG2E = math.log2(math.e)
NT = (((1,), (1,)), ((), ()))
NN = (((1,), (0,)), ((), ()))
F32 = jnp.float32
BF16 = jnp.bfloat16


def mm(a, b, dims=NN):
    return lax.dot_general(a, b, dims, preferred_element_type=F32)


def spread(t, head_lane):
    zero = jnp.zeros_like(t)
    return jnp.concatenate([jnp.where(head_lane == h, t, zero) for h in range(4)], 0)


def gather_diag(full, head_lane):
    out = full[0:64]
    for h in range(1, 4):
        out = jnp.where(head_lane == h, full[64 * h : 64 * h + 64], out)
    return out


TOKENS = 1024
HERE = pl.BlockSpec(memory_space=pltpu.VMEM)
F = 2 * D + 128


def right_half(shape):
    return lax.broadcasted_iota(jnp.int32, shape, 1) >= 4


def seam(a, b):
    return jnp.where(right_half(a.shape), a, b)


def tile_of(t, j):
    return t[:, 8 * j : 8 * j + 8, :]


def fold(t):
    t = t.astype(F32)
    return seam(pltpu.roll(t[6:12], 4, 1), t[0:6]).astype(BF16)


def unfold(t):
    t = t.astype(F32)
    return jnp.concatenate([t, pltpu.roll(t, 4, 1)], 0)


def pack_body(*refs):
    ins, (up, down, left, corner) = refs[:9], refs[9:]
    lane = 0
    for top, bottom, strip in (ins[0:3], ins[3:6], ins[6:9]):
        width = top.shape[-1]
        lanes = slice(lane, lane + width)
        lane += width
        for j in range(4):
            up[:, 8 * j : 8 * j + 8, lanes] = seam(tile_of(top, j), tile_of(top, j + 1))
        for j in range(3):
            down[:, 8 * j : 8 * j + 8, lanes] = seam(tile_of(bottom, j + 4), tile_of(bottom, j + 5))
        down[:, 24:32, lanes] = tile_of(bottom, 7)
        left[:, :, lanes] = fold(strip[0:12])
        corner[:, :, lanes] = tile_of(bottom, 0)


def pack_call(x, g, kb):
    specs = []
    for t in (x, g, kb):
        w = t.shape[-1]
        specs += [
            pl.BlockSpec((4, 64, w), lambda i: (0, 0, 0)),
            pl.BlockSpec((4, 64, w), lambda i: (3, 0, 0)),
            pl.BlockSpec((16, 8, w), lambda i: (0, 0, 0)),
        ]
    shapes = [(4, 32, F), (4, 32, F), (6, 8, F), (4, 8, F)]
    return pl.pallas_call(
        pack_body,
        grid=(1,),
        in_specs=specs,
        out_specs=[pl.BlockSpec(sh, lambda i: (0, 0, 0)) for sh in shapes],
        out_shape=[jax.ShapeDtypeStruct(sh, BF16) for sh in shapes],
        compiler_params=pltpu.CompilerParams(vmem_limit_bytes=60 << 20),
        cost_estimate=pl.CostEstimate(flops=0, bytes_accessed=4_000_000, transcendentals=0),
        name="pack",
    )(x, x, x, g, g, g, kb, kb, kb)


def window_pieces(src, below, above, right, corner, lanes):
    out = []
    right = unfold(right[:, :, lanes]).astype(BF16)
    for j in range(8):
        nxt = tile_of(src[4:12], j + 1) if j < 7 else right[4:12]
        out.append(seam(tile_of(src[4:12], j), nxt))
    for j in range(4):
        own = seam(tile_of(src[12:16], j), tile_of(src[12:16], j + 1))
        out.append(jnp.concatenate([own, tile_of(below, j)[:, :, lanes]], 0))
    for j in range(4):
        nxt = tile_of(src[0:4], j + 5) if j < 3 else right[0:4]
        own = seam(tile_of(src[0:4], j + 4), nxt)
        top = tile_of(above, j)[:, :, lanes]
        if j == 3:
            top = seam(top, corner[:, :, lanes])
        out.append(jnp.concatenate([top, own], 0))
    return out


def attn_body(core_ref, x_ref, g_ref, kb_ref, corner, right, below, above, wq_ref, wk_ref, wv_ref, wg_ref, wqkv_hbm, wo_hbm,
              attn_ref, gs_ref, up, down, side, edge, keep_ref, send_ref,
              mixed_ref, dq_ref, dk_ref, dv_ref, xw, wqkv, wo, sems, gw, bias, hid, hid_t, qs, ks, vs, gm, mix_t):

    loads = [
        pltpu.make_async_copy(wqkv_hbm, wqkv, sems.at[0]),
        pltpu.make_async_copy(wo_hbm, wo, sems.at[1]),
    ]

    @pl.when(pl.program_id(0) == 0)
    def _():
        for load in loads:
            load.start()
        halo = (below, above, right, corner)
        for w, t in enumerate(window_pieces(x_ref, *halo, slice(0, D))):
            xw[64 * w : 64 * w + 64, :] = t.astype(F32).reshape(64, D).astype(BF16)
        for w, t in enumerate(window_pieces(g_ref, *halo, slice(D, 2 * D))):
            gw[64 * w : 64 * w + 64, :] = t.astype(F32).reshape(64, D).astype(BF16)
        lane = lax.broadcasted_iota(jnp.int32, (64, 128), 1) % 64
        itself = lane == lax.broadcasted_iota(jnp.int32, (64, 128), 0)
        for w, t in enumerate(window_pieces(kb_ref, *halo, slice(2 * D, F))):
            keep = t.astype(F32).reshape(64, 128) > 0.5
            bias[64 * w : 64 * w + 64, :] = jnp.where(keep | itself, 0.0, -1e30)

        @pl.loop(0, TOKENS // 128)
        def _(i):
            rows = pl.ds(pl.multiple_of(i * 128, 128), 128)
            x = xw[rows, :].astype(F32)
            c = x - jnp.mean(x, -1, keepdims=True)
            inv = lax.rsqrt(jnp.mean(c * c, -1, keepdims=True) + EPS)
            n = c * inv
            hid[rows, :] = n.astype(BF16)
            hid_t[:, rows] = jnp.transpose(n).astype(BF16)

    group = pl.program_id(0)
    base = pl.multiple_of(group * GD, GD)
    cols = pl.ds(base, GD)
    h = hid[...]
    for w, out in ((wq_ref, qs), (wk_ref, ks), (wv_ref, vs)):
        out[...] = mm(h, w[...]).astype(BF16)
    gm[...] = mm(gw[...], wg_ref[...], NT).astype(BF16)

    head_lane = lax.broadcasted_iota(jnp.int32, (64, 128), 1) // 32

    U = 4
    TN = (((0,), (0,)), ((), ()))

    @pl.loop(0, 16 // U)
    def _(w):
        keys = []
        for u in range(U):
            rows = pl.ds(pl.multiple_of(w * 64 * U + 64 * u, 64), 64)
            for s in range(GD // 128):
                keys.append((rows, slice(128 * s, 128 * s + 128)))
        ch = [(qs[c], ks[c], vs[c], gm[c]) for c in keys]
        allow = []
        for u in range(U):
            bb = bias[keys[2 * u][0], :]
            allow += [jnp.concatenate([bb, bb], 1)] * 2
        qb = [spread(c[0], head_lane) for c in ch]
        sc = [mm(c[1], b, NT) for c, b in zip(ch, qb)]
        gb = [spread(c[3], head_lane) for c in ch]
        dp = [mm(c[2], b, NT) for c, b in zip(ch, gb)]
        ps, pbs, dbs = [], [], []
        for s, b in zip(sc, allow):
            s = s * (SCALE * LOG2E) + b
            e = jnp.exp2(s - jnp.max(s, 0, keepdims=True))
            p = e * (1.0 / jnp.sum(e, 0, keepdims=True))
            ps.append(p)
            pbs.append(p.astype(BF16))
        for p, d in zip(ps, dp):
            ds = p * ((d - jnp.sum(d * p, 0, keepdims=True)) * SCALE)
            dbs.append(ds.astype(BF16))
        dv = [mm(p, b) for p, b in zip(pbs, gb)]
        mx = [mm(p, c[2], TN) for p, c in zip(pbs, ch)]
        dk = [mm(d, b) for d, b in zip(dbs, qb)]
        dq = [mm(d, c[1], TN) for d, c in zip(dbs, ch)]
        for i, (rows, lanes) in enumerate(keys):
            c = rows, pl.ds(pl.multiple_of(base + lanes.start, 128), 128)
            dv_ref[c] = dv[i].astype(BF16)
            mixed_ref[c] = gather_diag(mx[i], head_lane).astype(BF16)
            dk_ref[c] = dk[i].astype(BF16)
            dq_ref[c] = gather_diag(dq[i], head_lane).astype(BF16)

    @pl.loop(0, TOKENS // 128)
    def _(i):
        rows = pl.ds(pl.multiple_of(i * 128, 128), 128)
        mix_t[:, rows] = jnp.transpose(mixed_ref[rows, cols].astype(F32)).astype(BF16)

    core = core_ref[0]
    for out, half in ((keep_ref, core), (send_ref, 1 - core)):
        h = hid_t[pl.ds(pl.multiple_of(half * 384, 128), 384), :]
        for p, t in enumerate((dq_ref, dk_ref, dv_ref)):
            out[0:384, GD * p : GD * p + GD] = mm(h, t[:, cols]).astype(BF16)
        m = mix_t[pl.ds(pl.multiple_of(half * 128, 128), 128), :]
        out[384:512, :] = mm(m, gw[...]).astype(BF16)

    @pl.when(group == 2)
    def _():
        for load in loads:
            load.wait()

        @pl.loop(0, 2)
        def _(i):
            rows = pl.ds(pl.multiple_of(i * 512, 512), 512)
            attn_ref[rows, :] = mm(mixed_ref[rows, :], wo[...]).astype(BF16)
            dh = mm(dq_ref[rows, :], wqkv[:, 0:768], NT)
            dh += mm(dk_ref[rows, :], wqkv[:, 768:1536], NT)
            dh += mm(dv_ref[rows, :], wqkv[:, 1536:2304], NT)
            x = xw[rows, :].astype(F32)
            c = x - jnp.mean(x, -1, keepdims=True)
            inv = lax.rsqrt(jnp.mean(c * c, -1, keepdims=True) + EPS)
            n = c * inv
            back = dh - jnp.mean(dh, -1, keepdims=True) - n * jnp.mean(dh * n, -1, keepdims=True)
            gs_ref[rows, :] = (inv * back).astype(BF16)

        for win, lanes in ((attn_ref, slice(0, D)), (gs_ref, slice(D, 2 * D))):
            piece = lambda w: win[64 * w : 64 * w + 64, :].astype(F32).reshape(8, 8, D).astype(BF16)
            for j in range(4):
                at = slice(8 * j, 8 * j + 8)
                up[:, at, lanes] = piece(12 + j)[0:4]
                down[:, at, lanes] = piece(8 + j)[4:8]
            side[:, :, lanes] = fold(jnp.concatenate([piece(15)[4:8], piece(7)], 0))
            edge[:, :, lanes] = piece(15)[0:4]


def attn_call(core, x, g, kb, halo, w_qkv, w_out):
    fixed = lambda t: pl.BlockSpec(t.shape, lambda i, c: (0,) * len(t.shape), pipeline_mode=pl.Buffered(1))
    wblock = lambda p: pl.BlockSpec((D, GD), lambda i, c: (0, 3 * p + i))
    half = pl.BlockSpec((512, D), lambda i, c: (i, 0))
    far = pl.BlockSpec(memory_space=pl.ANY)
    tok = jax.ShapeDtypeStruct((TOKENS, D), BF16)
    halves = jax.ShapeDtypeStruct((1536, D), BF16)
    borders = [jax.ShapeDtypeStruct((r, c, 2 * D), BF16) for r, c in ((4, 32), (4, 32), (6, 8), (4, 8))]
    return pl.pallas_call(
        attn_body,
        grid_spec=pltpu.PrefetchScalarGridSpec(
            num_scalar_prefetch=1,
            grid=(3,),
            in_specs=[fixed(t) for t in (x, g, kb, *halo)]
            + [wblock(0), wblock(1), wblock(2), pl.BlockSpec((GD, D), lambda i, c: (i, 0)), far, far],
            out_specs=[fixed(t) for t in (tok, tok, *borders)] + [half, half],
            scratch_shapes=[pltpu.VMEM((TOKENS, D), BF16)] * 5
            + [
                pltpu.VMEM((D, 3 * D), BF16),
                pltpu.VMEM((D, D), BF16),
                pltpu.SemaphoreType.DMA((2,)),
                pltpu.VMEM((TOKENS, D), BF16),
                pltpu.VMEM((TOKENS, 128), F32),
                pltpu.VMEM((TOKENS, D), BF16),
                pltpu.VMEM((D, TOKENS), BF16),
                pltpu.VMEM((TOKENS, GD), BF16),
                pltpu.VMEM((TOKENS, GD), BF16),
                pltpu.VMEM((TOKENS, GD), BF16),
                pltpu.VMEM((TOKENS, GD), BF16),
                pltpu.VMEM((GD, TOKENS), BF16),
            ],
        ),
        out_shape=[tok, tok, *borders, halves, halves],
        compiler_params=pltpu.CompilerParams(
            dimension_semantics=("arbitrary",), vmem_limit_bytes=56 << 20
        ),
        cost_estimate=pl.CostEstimate(
            flops=16_000_000_000, bytes_accessed=25_000_000, transcendentals=1_600_000
        ),
        name="attention",
    )(core, x, g, kb, *halo, w_qkv, w_qkv, w_qkv, w_out, w_qkv, w_out)


def merge_body(x_ref, g_ref, attn_ref, grad_ref, corner, left, below, above, out_ref, gin_ref):
    for src, win, dst, lanes in (
        (x_ref, attn_ref, out_ref, slice(0, D)),
        (g_ref, grad_ref, gin_ref, slice(D, 2 * D)),
    ):
        piece = lambda w: win[64 * w : 64 * w + 64, :].astype(F32).reshape(8, 8, D)
        far = lambda t, j: tile_of(t, j)[:, :, lanes].astype(F32)
        first = unfold(left[:, :, lanes])
        mids = [first[4:12]] + [piece(j) for j in range(8)]
        lows = [corner[:, :, lanes].astype(F32)] + [piece(8 + j)[0:4] for j in range(4)] + [far(below, j) for j in range(4)]
        tops = [first[0:4]] + [far(above, j) for j in range(4)] + [piece(12 + j)[4:8] for j in range(4)]
        for j in range(8):
            cols = slice(8 * j, 8 * j + 8)
            for rows, t in ((slice(4, 12), mids), (slice(12, 16), lows), (slice(0, 4), tops)):
                add = seam(t[j + 1], t[j])
                dst[rows, cols, :] = (src[rows, cols, :].astype(F32) + add).astype(BF16)


def merge_call(x, g, attn, grad, halo):
    tile = jax.ShapeDtypeStruct(x.shape, BF16)
    return pl.pallas_call(
        merge_body,
        out_shape=[tile, tile],
        compiler_params=pltpu.CompilerParams(vmem_limit_bytes=32 << 20),
        cost_estimate=pl.CostEstimate(flops=3_000_000, bytes_accessed=11_000_000, transcendentals=0),
        name="merge",
    )(x, g, attn, grad, *halo)


def combine_body(bits, keep, recv, *outs):
    for k in range(3):

        @pl.when(pl.program_id(0) == k)
        def _():
            for out, half in ((outs[k], bits[k]), (outs[3 + k], 1 - bits[k])):
                rows = pl.ds(pl.multiple_of(half * 256, 256), 256)
                out[...] = (keep[rows, :].astype(F32) + recv[rows, :].astype(F32)).astype(BF16)


def combine_call(bits, keep, recv):
    part = pl.BlockSpec((512, D), lambda i, c: (i, 0))
    half = pl.BlockSpec((256, D), lambda i, c: (0, 0), pipeline_mode=pl.Buffered(1))
    return pl.pallas_call(
        combine_body,
        grid_spec=pltpu.PrefetchScalarGridSpec(
            num_scalar_prefetch=1, grid=(3,), in_specs=[part] * 2, out_specs=[half] * 6
        ),
        out_shape=[jax.ShapeDtypeStruct((256, D), BF16)] * 6,
        compiler_params=pltpu.CompilerParams(
            dimension_semantics=("arbitrary",), vmem_limit_bytes=16 << 20
        ),
        cost_estimate=pl.CostEstimate(flops=1_200_000, bytes_accessed=7_000_000, transcendentals=0),
        name="combine",
    )(bits, keep, recv)


def join_body(bits, *refs):
    out = refs[-1]
    n = refs[0].shape[0]
    for k in range(len(refs) // 2):
        out[pl.ds(pl.multiple_of(n * (2 * k + bits[k]), n), n), :] = refs[2 * k][...]
        out[pl.ds(pl.multiple_of(n * (2 * k + 1 - bits[k]), n), n), :] = refs[2 * k + 1][...]


def join_call(bits, *halves):
    rows = len(halves) * halves[0].shape[0]
    return pl.pallas_call(
        join_body,
        grid_spec=pltpu.PrefetchScalarGridSpec(
            num_scalar_prefetch=1, grid=(1,), in_specs=[HERE] * len(halves), out_specs=HERE
        ),
        out_shape=jax.ShapeDtypeStruct((rows, D), BF16),
        compiler_params=pltpu.CompilerParams(vmem_limit_bytes=16 << 20),
        cost_estimate=pl.CostEstimate(flops=0, bytes_accessed=3072 * rows, transcendentals=0),
        name="join",
    )(bits, *halves)


def widen_body(core_ref, own, other, wqkv, wout):
    j = pl.program_id(0)
    core = core_ref[0]

    def put(src):
        for k in range(3):
            rows = pl.ds(pl.multiple_of(512 * k + j % 3 * 128, 128), 128)
            for p in range(3):
                wqkv[:, D * p + GD * k : D * p + GD * k + GD] = src[rows, GD * p : GD * p + GD].astype(F32)

    @pl.when((j < 6) & (j // 3 == core))
    def _():
        put(own)

    @pl.when((j < 6) & (j // 3 != core))
    def _():
        put(other)

    @pl.when(j == 6)
    def _():
        for src, half in ((own, core), (other, 1 - core)):
            for k in range(3):
                rows = pl.ds(pl.multiple_of(GD * k + half * 128, 128), 128)
                wout[rows, :] = src[512 * k + 384 : 512 * k + 512, :].astype(F32)


def widen_call(core, own, other):
    return pl.pallas_call(
        widen_body,
        grid_spec=pltpu.PrefetchScalarGridSpec(
            num_scalar_prefetch=1,
            grid=(7,),
            in_specs=[HERE] * 2,
            out_specs=[
                pl.BlockSpec((128, 3 * D), lambda j, c: (jnp.minimum(j, 5), 0)),
                pl.BlockSpec((D, D), lambda j, c: (0, 0)),
            ],
        ),
        out_shape=[jax.ShapeDtypeStruct((D, 3 * D), F32), jax.ShapeDtypeStruct((D, D), F32)],
        compiler_params=pltpu.CompilerParams(
            dimension_semantics=("arbitrary",), vmem_limit_bytes=32 << 20
        ),
        cost_estimate=pl.CostEstimate(flops=0, bytes_accessed=14_000_000, transcendentals=0),
        name="widen",
    )(core, own, other)


AXES = ("gx", "gy")


def place(i):
    gx, gy = divmod(i, 8)
    z_hi, y, core = gx // 8, gx // 2 % 4, gx % 2
    z_lo, x = divmod(gy, 4)
    return {"core": core, "x": x, "y": y, "z": 2 * z_hi + z_lo}


def number(d):
    z_hi, z_lo = divmod(d["z"], 2)
    return ((z_hi * 4 + d["y"]) * 2 + d["core"]) * 8 + z_lo * 4 + d["x"]


def exchange(v, axis, first):
    pairs = []
    for i in range(128):
        d = place(i)
        if axis == "core":
            d["core"] ^= 1
        elif (d["core"] == 0) == first:
            d[axis] ^= 1
        else:
            d[axis] = 3 - d[axis]
        pairs.append((i, number(d)))
    return lax.ppermute(v, AXES, pairs)


def half_of(axis, first):
    gx, gy = lax.axis_index("gx"), lax.axis_index("gy")
    core = gx % 2
    if axis == "core":
        return core
    p = {"x": gy % 4, "y": gx // 2 % 4, "z": gx // 8 * 2 + gy // 4}[axis]
    inner = ((p == 1) | (p == 2)).astype(jnp.int32)
    upper = (p >= 2).astype(jnp.int32)
    return jnp.where((core == 0) == first, inner, upper)


def add(a, b):
    return (a.astype(F32) + b.astype(F32)).astype(BF16)


def scatter_half(v, axis, first=True):
    n = v.shape[0] // 2
    b = half_of(axis, first)
    keep = lax.dynamic_slice_in_dim(v, b * n, n, 0)
    send = lax.dynamic_slice_in_dim(v, (1 - b) * n, n, 0)
    return add(keep, exchange(send, axis, first))


def total(keep, send):
    axes = [["xyz"[(k + s) % 3] for s in range(3)] for k in range(3)]
    recv = exchange(send, "core", True)
    bits = jnp.stack([half_of(a[0], True) for a in axes]).astype(jnp.int32)
    halves = combine_call(bits, keep, recv)
    parts = [add(halves[k], exchange(halves[3 + k], a[0], True)) for k, a in enumerate(axes)]
    parts = [scatter_half(p, a[1]) for p, a in zip(parts, axes)]
    for axis, first in ((2, True), (0, False), (1, False), (2, False)):
        parts = [add(p, exchange(p, a[axis], first)) for p, a in zip(parts, axes)]
    second = [half_of(a[1], True).astype(jnp.int32).reshape(1) for a in axes]
    parts = [join_call(b, p, exchange(p, a[1], True)) for b, p, a in zip(second, parts, axes)]
    halves = []
    for p, a in zip(parts, axes):
        halves += [p, exchange(p, a[0], True)]
    return join_call(bits, *halves)


def shift(v, d_gy, d_gx):
    pairs = []
    for gx in range(16):
        for gy in range(8):
            pairs.append((gx * 8 + gy, (gx + d_gx) % 16 * 8 + (gy + d_gy) % 8))
    return lax.ppermute(v, AXES, pairs)


def local(slide_tokens, tissue, grad_tokens, w_qkv, w_out):
    kb = jnp.broadcast_to(tissue.astype(BF16)[..., None], tissue.shape + (128,))
    core = (lax.axis_index("gx") % 2).astype(jnp.int32).reshape(1)
    up, down, left, corner = pack_call(slide_tokens, grad_tokens, kb)
    halo = (shift(corner, 1, -1), shift(left, 0, -1), shift(up, -1, 0), shift(down, 1, 0))
    attn, grad, up, down, side, edge, keep, send = attn_call(
        core, slide_tokens, grad_tokens, kb, halo, w_qkv, w_out
    )
    own = total(keep, send)

    own, (up, down, side, edge) = lax.optimization_barrier((own, (up, down, side, edge)))
    halo = (shift(edge, -1, 1), shift(side, 0, 1), shift(up, -1, 0), shift(down, 1, 0))
    grads = widen_call(core, own, exchange(own, "core", True))
    halo, grads = lax.optimization_barrier((halo, tuple(grads)))
    block_out, grad_in = merge_call(slide_tokens, grad_tokens, attn, grad, halo)
    return block_out, grad_in, *grads


def solution(mesh):
    tile = P("gy", "gx", None)
    return jax.shard_map(
        local,
        mesh=mesh,
        in_specs=(tile, P("gy", "gx"), tile, P(), P()),
        out_specs=(tile, tile, P(), P()),
        check_vma=False,
    )
```

```python
import functools
import math
import jax
import jax.numpy as jnp
from jax import lax
from jax.experimental import pallas as pl
from jax.experimental.pallas import tpu as pltpu
from jax.sharding import PartitionSpec as P

HEADS = 24
WIN = 8
SHIFT = 4
D = 768
GD = 256
EPS = 1e-05
SCALE = 1.0 / math.sqrt(32)
LOG2E = math.log2(math.e)
NT = (((1,), (1,)), ((), ()))
NN = (((1,), (0,)), ((), ()))
F32 = jnp.float32
BF16 = jnp.bfloat16


def mm(a, b, dims=NN):
    return lax.dot_general(a, b, dims, preferred_element_type=F32)


def spread(t, head_lane):
    zero = jnp.zeros_like(t)
    return jnp.concatenate([jnp.where(head_lane == h, t, zero) for h in range(4)], 0)


def gather_diag(full, head_lane):
    out = full[0:64]
    for h in range(1, 4):
        out = jnp.where(head_lane == h, full[64 * h : 64 * h + 64], out)
    return out


TOKENS = 1024
HERE = pl.BlockSpec(memory_space=pltpu.VMEM)
F = 2 * D + 128


def right_half(shape):
    return lax.broadcasted_iota(jnp.int32, shape, 1) >= 4


def seam(a, b):
    return jnp.where(right_half(a.shape), a, b)


def tile_of(t, j):
    return t[:, 8 * j : 8 * j + 8, :]


def fold(t):
    t = t.astype(F32)
    return seam(pltpu.roll(t[6:12], 4, 1), t[0:6]).astype(BF16)


def unfold(t):
    t = t.astype(F32)
    return jnp.concatenate([t, pltpu.roll(t, 4, 1)], 0)


def pack_body(*refs):
    ins, (up, down, left, corner) = refs[:9], refs[9:]
    lane = 0
    for top, bottom, strip in (ins[0:3], ins[3:6], ins[6:9]):
        width = top.shape[-1]
        lanes = slice(lane, lane + width)
        lane += width
        for j in range(4):
            up[:, 8 * j : 8 * j + 8, lanes] = seam(tile_of(top, j), tile_of(top, j + 1))
        for j in range(3):
            down[:, 8 * j : 8 * j + 8, lanes] = seam(tile_of(bottom, j + 4), tile_of(bottom, j + 5))
        down[:, 24:32, lanes] = tile_of(bottom, 7)
        left[:, :, lanes] = fold(strip[0:12])
        corner[:, :, lanes] = tile_of(bottom, 0)


def pack_call(x, g, kb):
    specs = []
    for t in (x, g, kb):
        w = t.shape[-1]
        specs += [
            pl.BlockSpec((4, 64, w), lambda i: (0, 0, 0)),
            pl.BlockSpec((4, 64, w), lambda i: (3, 0, 0)),
            pl.BlockSpec((16, 8, w), lambda i: (0, 0, 0)),
        ]
    shapes = [(4, 32, F), (4, 32, F), (6, 8, F), (4, 8, F)]
    return pl.pallas_call(
        pack_body,
        grid=(1,),
        in_specs=specs,
        out_specs=[pl.BlockSpec(sh, lambda i: (0, 0, 0)) for sh in shapes],
        out_shape=[jax.ShapeDtypeStruct(sh, BF16) for sh in shapes],
        compiler_params=pltpu.CompilerParams(vmem_limit_bytes=60 << 20),
        cost_estimate=pl.CostEstimate(flops=0, bytes_accessed=4_000_000, transcendentals=0),
        name="pack",
    )(x, x, x, g, g, g, kb, kb, kb)


def window_pieces(src, below, above, right, corner, lanes):
    out = []
    right = unfold(right[:, :, lanes]).astype(BF16)
    for j in range(8):
        nxt = tile_of(src[4:12], j + 1) if j < 7 else right[4:12]
        out.append(seam(tile_of(src[4:12], j), nxt))
    for j in range(4):
        own = seam(tile_of(src[12:16], j), tile_of(src[12:16], j + 1))
        out.append(jnp.concatenate([own, tile_of(below, j)[:, :, lanes]], 0))
    for j in range(4):
        nxt = tile_of(src[0:4], j + 5) if j < 3 else right[0:4]
        own = seam(tile_of(src[0:4], j + 4), nxt)
        top = tile_of(above, j)[:, :, lanes]
        if j == 3:
            top = seam(top, corner[:, :, lanes])
        out.append(jnp.concatenate([top, own], 0))
    return out


def attn_body(core_ref, x_ref, g_ref, kb_ref, corner, right, below, above, wq_ref, wk_ref, wv_ref, wg_ref, wqkv_hbm, wo_hbm,
              attn_ref, gs_ref, up, down, side, edge, keep_ref, send_ref,
              mixed_ref, dq_ref, dk_ref, dv_ref, xw, wqkv, wo, sems, gw, bias, hid, hid_t, qs, ks, vs, gm, mix_t):

    loads = [
        pltpu.make_async_copy(wqkv_hbm, wqkv, sems.at[0]),
        pltpu.make_async_copy(wo_hbm, wo, sems.at[1]),
    ]

    @pl.when(pl.program_id(0) == 0)
    def _():
        for load in loads:
            load.start()
        halo = (below, above, right, corner)
        for w, t in enumerate(window_pieces(x_ref, *halo, slice(0, D))):
            xw[64 * w : 64 * w + 64, :] = t.astype(F32).reshape(64, D).astype(BF16)
        for w, t in enumerate(window_pieces(g_ref, *halo, slice(D, 2 * D))):
            gw[64 * w : 64 * w + 64, :] = t.astype(F32).reshape(64, D).astype(BF16)
        lane = lax.broadcasted_iota(jnp.int32, (64, 128), 1) % 64
        itself = lane == lax.broadcasted_iota(jnp.int32, (64, 128), 0)
        for w, t in enumerate(window_pieces(kb_ref, *halo, slice(2 * D, F))):
            keep = t.astype(F32).reshape(64, 128) > 0.5
            bias[64 * w : 64 * w + 64, :] = jnp.where(keep | itself, 0.0, -1e30)

        @pl.loop(0, TOKENS // 128)
        def _(i):
            rows = pl.ds(pl.multiple_of(i * 128, 128), 128)
            x = xw[rows, :].astype(F32)
            c = x - jnp.mean(x, -1, keepdims=True)
            inv = lax.rsqrt(jnp.mean(c * c, -1, keepdims=True) + EPS)
            n = c * inv
            hid[rows, :] = n.astype(BF16)
            hid_t[:, rows] = jnp.transpose(n).astype(BF16)

    group = pl.program_id(0)
    base = pl.multiple_of(group * GD, GD)
    cols = pl.ds(base, GD)
    h = hid[...]
    for w, out in ((wq_ref, qs), (wk_ref, ks), (wv_ref, vs)):
        out[...] = mm(h, w[...]).astype(BF16)
    gm[...] = mm(gw[...], wg_ref[...], NT).astype(BF16)

    head_lane = lax.broadcasted_iota(jnp.int32, (64, 128), 1) // 32

    U = 4
    TN = (((0,), (0,)), ((), ()))

    @pl.loop(0, 16 // U)
    def _(w):
        keys = []
        for u in range(U):
            rows = pl.ds(pl.multiple_of(w * 64 * U + 64 * u, 64), 64)
            for s in range(GD // 128):
                keys.append((rows, slice(128 * s, 128 * s + 128)))
        ch = [(qs[c], ks[c], vs[c], gm[c]) for c in keys]
        allow = []
        for u in range(U):
            bb = bias[keys[2 * u][0], :]
            allow += [jnp.concatenate([bb, bb], 1)] * 2
        qb = [spread(c[0], head_lane) for c in ch]
        sc = [mm(c[1], b, NT) for c, b in zip(ch, qb)]
        gb = [spread(c[3], head_lane) for c in ch]
        dp = [mm(c[2], b, NT) for c, b in zip(ch, gb)]
        ps, pbs, dbs = [], [], []
        for s, b in zip(sc, allow):
            s = s * (SCALE * LOG2E) + b
            e = jnp.exp2(s - jnp.max(s, 0, keepdims=True))
            p = e * (1.0 / jnp.sum(e, 0, keepdims=True))
            ps.append(p)
            pbs.append(p.astype(BF16))
        for p, d in zip(ps, dp):
            ds = p * ((d - jnp.sum(d * p, 0, keepdims=True)) * SCALE)
            dbs.append(ds.astype(BF16))
        dv = [mm(p, b) for p, b in zip(pbs, gb)]
        mx = [mm(p, c[2], TN) for p, c in zip(pbs, ch)]
        dk = [mm(d, b) for d, b in zip(dbs, qb)]
        dq = [mm(d, c[1], TN) for d, c in zip(dbs, ch)]
        for i, (rows, lanes) in enumerate(keys):
            c = rows, pl.ds(pl.multiple_of(base + lanes.start, 128), 128)
            dv_ref[c] = dv[i].astype(BF16)
            mixed_ref[c] = gather_diag(mx[i], head_lane).astype(BF16)
            dk_ref[c] = dk[i].astype(BF16)
            dq_ref[c] = gather_diag(dq[i], head_lane).astype(BF16)

    @pl.loop(0, TOKENS // 128)
    def _(i):
        rows = pl.ds(pl.multiple_of(i * 128, 128), 128)
        mix_t[:, rows] = jnp.transpose(mixed_ref[rows, cols].astype(F32)).astype(BF16)

    core = core_ref[0]
    for out, half in ((keep_ref, core), (send_ref, 1 - core)):
        h = hid_t[pl.ds(pl.multiple_of(half * 384, 128), 384), :]
        for p, t in enumerate((dq_ref, dk_ref, dv_ref)):
            out[0:384, GD * p : GD * p + GD] = mm(h, t[:, cols]).astype(BF16)
        m = mix_t[pl.ds(pl.multiple_of(half * 128, 128), 128), :]
        out[384:512, :] = mm(m, gw[...]).astype(BF16)

    @pl.when(group == 2)
    def _():
        for load in loads:
            load.wait()

        for i in range(2):
            rows = slice(512 * i, 512 * i + 512)
            attn_ref[rows, :] = mm(mixed_ref[rows, :], wo[...]).astype(BF16)
            dh = mm(dq_ref[rows, :], wqkv[:, 0:768], NT)
            dh += mm(dk_ref[rows, :], wqkv[:, 768:1536], NT)
            dh += mm(dv_ref[rows, :], wqkv[:, 1536:2304], NT)
            x = xw[rows, :].astype(F32)
            c = x - jnp.mean(x, -1, keepdims=True)
            inv = lax.rsqrt(jnp.mean(c * c, -1, keepdims=True) + EPS)
            n = c * inv
            back = dh - jnp.mean(dh, -1, keepdims=True) - n * jnp.mean(dh * n, -1, keepdims=True)
            gs_ref[rows, :] = (inv * back).astype(BF16)

        for win, lanes in ((attn_ref, slice(0, D)), (gs_ref, slice(D, 2 * D))):
            piece = lambda w: win[64 * w : 64 * w + 64, :].astype(F32).reshape(8, 8, D).astype(BF16)
            for j in range(4):
                at = slice(8 * j, 8 * j + 8)
                up[:, at, lanes] = piece(12 + j)[0:4]
                down[:, at, lanes] = piece(8 + j)[4:8]
            side[:, :, lanes] = fold(jnp.concatenate([piece(15)[4:8], piece(7)], 0))
            edge[:, :, lanes] = piece(15)[0:4]


def attn_call(core, x, g, kb, halo, w_qkv, w_out):
    fixed = lambda t: pl.BlockSpec(t.shape, lambda i, c: (0,) * len(t.shape), pipeline_mode=pl.Buffered(1))
    wblock = lambda p: pl.BlockSpec((D, GD), lambda i, c: (0, 3 * p + i))
    half = pl.BlockSpec((512, D), lambda i, c: (i, 0))
    far = pl.BlockSpec(memory_space=pl.ANY)
    tok = jax.ShapeDtypeStruct((TOKENS, D), BF16)
    halves = jax.ShapeDtypeStruct((1536, D), BF16)
    borders = [jax.ShapeDtypeStruct((r, c, 2 * D), BF16) for r, c in ((4, 32), (4, 32), (6, 8), (4, 8))]
    return pl.pallas_call(
        attn_body,
        grid_spec=pltpu.PrefetchScalarGridSpec(
            num_scalar_prefetch=1,
            grid=(3,),
            in_specs=[fixed(t) for t in (x, g, kb, *halo)]
            + [wblock(0), wblock(1), wblock(2), pl.BlockSpec((GD, D), lambda i, c: (i, 0)), far, far],
            out_specs=[fixed(t) for t in (tok, tok, *borders)] + [half, half],
            scratch_shapes=[pltpu.VMEM((TOKENS, D), BF16)] * 5
            + [
                pltpu.VMEM((D, 3 * D), BF16),
                pltpu.VMEM((D, D), BF16),
                pltpu.SemaphoreType.DMA((2,)),
                pltpu.VMEM((TOKENS, D), BF16),
                pltpu.VMEM((TOKENS, 128), F32),
                pltpu.VMEM((TOKENS, D), BF16),
                pltpu.VMEM((D, TOKENS), BF16),
                pltpu.VMEM((TOKENS, GD), BF16),
                pltpu.VMEM((TOKENS, GD), BF16),
                pltpu.VMEM((TOKENS, GD), BF16),
                pltpu.VMEM((TOKENS, GD), BF16),
                pltpu.VMEM((GD, TOKENS), BF16),
            ],
        ),
        out_shape=[tok, tok, *borders, halves, halves],
        compiler_params=pltpu.CompilerParams(
            dimension_semantics=("arbitrary",), vmem_limit_bytes=56 << 20
        ),
        cost_estimate=pl.CostEstimate(
            flops=16_000_000_000, bytes_accessed=25_000_000, transcendentals=1_600_000
        ),
        name="attention",
    )(core, x, g, kb, *halo, w_qkv, w_qkv, w_qkv, w_out, w_qkv, w_out)


def merge_body(x_ref, g_ref, attn_ref, grad_ref, corner, left, below, above, out_ref, gin_ref):
    for src, win, dst, lanes in (
        (x_ref, attn_ref, out_ref, slice(0, D)),
        (g_ref, grad_ref, gin_ref, slice(D, 2 * D)),
    ):
        piece = lambda w: win[64 * w : 64 * w + 64, :].astype(F32).reshape(8, 8, D)
        far = lambda t, j: tile_of(t, j)[:, :, lanes].astype(F32)
        first = unfold(left[:, :, lanes])
        mids = [first[4:12]] + [piece(j) for j in range(8)]
        lows = [corner[:, :, lanes].astype(F32)] + [piece(8 + j)[0:4] for j in range(4)] + [far(below, j) for j in range(4)]
        tops = [first[0:4]] + [far(above, j) for j in range(4)] + [piece(12 + j)[4:8] for j in range(4)]
        for j in range(8):
            cols = slice(8 * j, 8 * j + 8)
            for rows, t in ((slice(4, 12), mids), (slice(12, 16), lows), (slice(0, 4), tops)):
                add = seam(t[j + 1], t[j])
                dst[rows, cols, :] = (src[rows, cols, :].astype(F32) + add).astype(BF16)


def merge_call(x, g, attn, grad, halo):
    tile = jax.ShapeDtypeStruct(x.shape, BF16)
    return pl.pallas_call(
        merge_body,
        out_shape=[tile, tile],
        compiler_params=pltpu.CompilerParams(vmem_limit_bytes=32 << 20),
        cost_estimate=pl.CostEstimate(flops=3_000_000, bytes_accessed=11_000_000, transcendentals=0),
        name="merge",
    )(x, g, attn, grad, *halo)


def combine_body(bits, keep, recv, *outs):
    for k in range(3):

        @pl.when(pl.program_id(0) == k)
        def _():
            for out, half in ((outs[k], bits[k]), (outs[3 + k], 1 - bits[k])):
                rows = pl.ds(pl.multiple_of(half * 256, 256), 256)
                out[...] = (keep[rows, :].astype(F32) + recv[rows, :].astype(F32)).astype(BF16)


def combine_call(bits, keep, recv):
    part = pl.BlockSpec((512, D), lambda i, c: (i, 0))
    half = pl.BlockSpec((256, D), lambda i, c: (0, 0), pipeline_mode=pl.Buffered(1))
    return pl.pallas_call(
        combine_body,
        grid_spec=pltpu.PrefetchScalarGridSpec(
            num_scalar_prefetch=1, grid=(3,), in_specs=[part] * 2, out_specs=[half] * 6
        ),
        out_shape=[jax.ShapeDtypeStruct((256, D), BF16)] * 6,
        compiler_params=pltpu.CompilerParams(
            dimension_semantics=("arbitrary",), vmem_limit_bytes=16 << 20
        ),
        cost_estimate=pl.CostEstimate(flops=1_200_000, bytes_accessed=7_000_000, transcendentals=0),
        name="combine",
    )(bits, keep, recv)


def join_body(bits, *refs):
    out = refs[-1]
    n = refs[0].shape[0]
    for k in range(len(refs) // 2):
        out[pl.ds(pl.multiple_of(n * (2 * k + bits[k]), n), n), :] = refs[2 * k][...]
        out[pl.ds(pl.multiple_of(n * (2 * k + 1 - bits[k]), n), n), :] = refs[2 * k + 1][...]


def join_call(bits, *halves):
    rows = len(halves) * halves[0].shape[0]
    return pl.pallas_call(
        join_body,
        grid_spec=pltpu.PrefetchScalarGridSpec(
            num_scalar_prefetch=1, grid=(1,), in_specs=[HERE] * len(halves), out_specs=HERE
        ),
        out_shape=jax.ShapeDtypeStruct((rows, D), BF16),
        compiler_params=pltpu.CompilerParams(vmem_limit_bytes=16 << 20),
        cost_estimate=pl.CostEstimate(flops=0, bytes_accessed=3072 * rows, transcendentals=0),
        name="join",
    )(bits, *halves)


def widen_body(core_ref, own, other, wqkv, wout):
    j = pl.program_id(0)
    core = core_ref[0]

    def put(src):
        for k in range(3):
            rows = pl.ds(pl.multiple_of(512 * k + j % 3 * 128, 128), 128)
            for p in range(3):
                wqkv[:, D * p + GD * k : D * p + GD * k + GD] = src[rows, GD * p : GD * p + GD].astype(F32)

    @pl.when((j < 6) & (j // 3 == core))
    def _():
        put(own)

    @pl.when((j < 6) & (j // 3 != core))
    def _():
        put(other)

    @pl.when(j == 6)
    def _():
        for src, half in ((own, core), (other, 1 - core)):
            for k in range(3):
                rows = pl.ds(pl.multiple_of(GD * k + half * 128, 128), 128)
                wout[rows, :] = src[512 * k + 384 : 512 * k + 512, :].astype(F32)


def widen_call(core, own, other):
    return pl.pallas_call(
        widen_body,
        grid_spec=pltpu.PrefetchScalarGridSpec(
            num_scalar_prefetch=1,
            grid=(7,),
            in_specs=[HERE] * 2,
            out_specs=[
                pl.BlockSpec((128, 3 * D), lambda j, c: (jnp.minimum(j, 5), 0)),
                pl.BlockSpec((D, D), lambda j, c: (0, 0)),
            ],
        ),
        out_shape=[jax.ShapeDtypeStruct((D, 3 * D), F32), jax.ShapeDtypeStruct((D, D), F32)],
        compiler_params=pltpu.CompilerParams(
            dimension_semantics=("arbitrary",), vmem_limit_bytes=32 << 20
        ),
        cost_estimate=pl.CostEstimate(flops=0, bytes_accessed=14_000_000, transcendentals=0),
        name="widen",
    )(core, own, other)


AXES = ("gx", "gy")


def place(i):
    gx, gy = divmod(i, 8)
    z_hi, y, core = gx // 8, gx // 2 % 4, gx % 2
    z_lo, x = divmod(gy, 4)
    return {"core": core, "x": x, "y": y, "z": 2 * z_hi + z_lo}


def number(d):
    z_hi, z_lo = divmod(d["z"], 2)
    return ((z_hi * 4 + d["y"]) * 2 + d["core"]) * 8 + z_lo * 4 + d["x"]


def exchange(v, axis, first):
    pairs = []
    for i in range(128):
        d = place(i)
        if axis == "core":
            d["core"] ^= 1
        elif (d["core"] == 0) == first:
            d[axis] ^= 1
        else:
            d[axis] = 3 - d[axis]
        pairs.append((i, number(d)))
    return lax.ppermute(v, AXES, pairs)


def half_of(axis, first):
    gx, gy = lax.axis_index("gx"), lax.axis_index("gy")
    core = gx % 2
    if axis == "core":
        return core
    p = {"x": gy % 4, "y": gx // 2 % 4, "z": gx // 8 * 2 + gy // 4}[axis]
    inner = ((p == 1) | (p == 2)).astype(jnp.int32)
    upper = (p >= 2).astype(jnp.int32)
    return jnp.where((core == 0) == first, inner, upper)


def add(a, b):
    return (a.astype(F32) + b.astype(F32)).astype(BF16)


def scatter_half(v, axis, first=True):
    n = v.shape[0] // 2
    b = half_of(axis, first)
    keep = lax.dynamic_slice_in_dim(v, b * n, n, 0)
    send = lax.dynamic_slice_in_dim(v, (1 - b) * n, n, 0)
    return add(keep, exchange(send, axis, first))


def total(keep, send):
    axes = [["xyz"[(k + s) % 3] for s in range(3)] for k in range(3)]
    recv = exchange(send, "core", True)
    bits = jnp.stack([half_of(a[0], True) for a in axes]).astype(jnp.int32)
    halves = combine_call(bits, keep, recv)
    parts = [add(halves[k], exchange(halves[3 + k], a[0], True)) for k, a in enumerate(axes)]
    parts = [scatter_half(p, a[1]) for p, a in zip(parts, axes)]
    for axis, first in ((2, True), (0, False), (1, False), (2, False)):
        parts = [add(p, exchange(p, a[axis], first)) for p, a in zip(parts, axes)]
    second = [half_of(a[1], True).astype(jnp.int32).reshape(1) for a in axes]
    parts = [join_call(b, p, exchange(p, a[1], True)) for b, p, a in zip(second, parts, axes)]
    halves = []
    for p, a in zip(parts, axes):
        halves += [p, exchange(p, a[0], True)]
    return join_call(bits, *halves)


def shift(v, d_gy, d_gx):
    pairs = []
    for gx in range(16):
        for gy in range(8):
            pairs.append((gx * 8 + gy, (gx + d_gx) % 16 * 8 + (gy + d_gy) % 8))
    return lax.ppermute(v, AXES, pairs)


def local(slide_tokens, tissue, grad_tokens, w_qkv, w_out):
    kb = jnp.broadcast_to(tissue[..., None], tissue.shape + (128,)).astype(BF16)
    core = (lax.axis_index("gx") % 2).astype(jnp.int32).reshape(1)
    up, down, left, corner = pack_call(slide_tokens, grad_tokens, kb)
    halo = (shift(corner, 1, -1), shift(left, 0, -1), shift(up, -1, 0), shift(down, 1, 0))
    attn, grad, up, down, side, edge, keep, send = attn_call(
        core, slide_tokens, grad_tokens, kb, halo, w_qkv, w_out
    )
    own = total(keep, send)

    own, (up, down, side, edge) = lax.optimization_barrier((own, (up, down, side, edge)))
    halo = (shift(edge, -1, 1), shift(side, 0, 1), shift(up, -1, 0), shift(down, 1, 0))
    grads = widen_call(core, own, exchange(own, "core", True))
    halo, grads = lax.optimization_barrier((halo, tuple(grads)))
    block_out, grad_in = merge_call(slide_tokens, grad_tokens, attn, grad, halo)
    return block_out, grad_in, *grads


def solution(mesh):
    tile = P("gy", "gx", None)
    return jax.shard_map(
        local,
        mesh=mesh,
        in_specs=(tile, P("gy", "gx"), tile, P(), P()),
        out_specs=(tile, tile, P(), P()),
        check_vma=False,
    )
```
